256 devices in a mesh: group: 8 (over z), date: 32 (over x, y, core).
Axes of the slice: x: 4, y: 4, z: 8, core: 2. Of those that a mesh axis runs over, the one named last changes fastest.
Arguments:
- pixels: bfloat16 [13, 24, 512, 4096], P(None, None, 'date', 'group'), may hold values from -6 to 6
- counts: int32 [512, 4096], P('date', 'group'), may hold values from 1 to 24
- edge_pixels: bfloat16 [13, 8, 512, 512], P(None, None, 'date', 'group'), may hold values from 1.5 to 6
- edge_mask: int32 [8, 512, 512], P(None, 'date', 'group'), may hold values 0 or 1
- straddle_lot: int32 [512], P('group'), may hold values from 0 to 511, as said below
- date_days: int32 [512], replicated, may hold values from 0 to 1022, as said below
- w_first: bfloat16 [32, 13], replicated, may hold values from -1.75 to 1.75
- b_first: float32 [32], replicated, may hold values from -3 to 3
- w_second: bfloat16 [128, 32], replicated, may hold values from -1 to 1
- b_second: float32 [128], replicated, may hold values from -3 to 3
- w_pool: bfloat16 [256, 128], replicated, may hold values from -0.375 to 0.375
- b_pool: float32 [128], replicated, may hold values from -3 to 3
- ln_one: float32 [128], replicated, may hold values from 0.5 to 1.5
- w_query: bfloat16 [128, 128], replicated
- w_key: bfloat16 [128, 128], replicated
- w_value: bfloat16 [128, 128], replicated, may hold values from -0.5 to 0.5
- w_out: bfloat16 [128, 128], replicated, may hold values from -0.5 to 0.5
- ln_two: float32 [128], replicated, may hold values from 0.5 to 1.5
- w_up: bfloat16 [128, 512], replicated, may hold values from -0.5 to 0.5
- w_down: bfloat16 [512, 128], replicated, may hold values from -0.25 to 0.25
Outputs:
- encoded: bfloat16 [512, 4096, 128], P(None, ('group', 'date'))
The draws below stay inside these ranges and needn't reach their ends.
Inputs may be any that keep to these rules, and one draw needn't show every extreme that they name: `straddle_lot`: within each lot group's 64 entries the lots are distinct. `date_days`: strictly increasing day numbers; the first is 0 and the last is 1022.
All inputs are finite; a program needn't handle non-finite values. No bound on the sum of `edge_mask` on one device may be relied on, other than what follows from the above.
Results may differ from the reference program's by a relative error of at most 0.012.
The reference program's roundings to bfloat16 on the way count: a program that leaves them out, or rounds other values in their place, can miss the bound.
Values may be sent and summed in bfloat16 or wider, within the bound.
No kernel may reach another device: no remote copies, remote signals or barrier semaphores. Data moves between devices by JAX's collectives and lax.ppermute only.
A program may use at most 128 MiB of HBM per device.

```python
import math
import jax
import jax.numpy as jnp
from jax import lax

BANDS = 13
PIX = 24
EDGE = 8
H1 = 32
PFEAT = 128
EMB = 128
HEADS = 4
FFN = 512
LOTS_G = 512
STR_G = 64
DATES = 512
LOTS = 4096
STR_TOTAL = 512
N_GROUP = 8


def draw_straddle_lot(key, part):
    group_keys = jax.random.split(key, N_GROUP)
    shuffled = jax.vmap(lambda one_key: jax.random.permutation(one_key, STR_G))(group_keys)
    stride = LOTS_G // STR_G
    jitter = jax.random.randint(jax.random.fold_in(key, 3), (N_GROUP, STR_G), 0, stride)
    first_group = jnp.arange(N_GROUP)[:, None] == 0
    jitter = jnp.where(first_group & (shuffled == 0), 0, jitter)
    jitter = jnp.where(first_group & (shuffled == STR_G - 1), stride - 1, jitter)
    return (shuffled * stride + jitter).reshape(-1).astype(jnp.int32)


def draw_date_days(key, part):
    last_day = 2 * (DATES - 1)
    candidate_count = last_day - 1
    raw_scores = jax.random.randint(key, (candidate_count,), 0, 2 ** 19)
    distinct_scores = raw_scores * candidate_count + jnp.arange(candidate_count, dtype=jnp.int32)
    picked_ids = jax.lax.top_k(distinct_scores, DATES - 2)[1]
    middle_days = jnp.sort(picked_ids + 1)
    first_day = jnp.zeros((1,), jnp.int32)
    final_day = jnp.full((1,), last_day, jnp.int32)
    return jnp.concatenate([first_day, middle_days.astype(jnp.int32), final_day]).astype(jnp.int32)


def query_key_pair(key):
    base_key = jax.random.normal(jax.random.fold_in(key, 11), (EMB, EMB), jnp.float32) / math.sqrt(EMB)
    query_noise = jax.random.normal(jax.random.fold_in(key, 12), (EMB, EMB), jnp.float32) / math.sqrt(EMB)
    queries = query_noise
    return (queries, base_key)


def draw_w_query(key, part):
    return query_key_pair(key)[0].astype(jnp.bfloat16)


def draw_w_key(key, part):
    return query_key_pair(key)[1].astype(jnp.bfloat16)


def touch_ends(values, rng, least, largest):
    index_at = [jax.random.randint(jax.random.fold_in(rng, axis), (), 0, length) for axis, length in enumerate(values.shape)]
    widest = values.shape.index(max(values.shape))
    neighbour = index_at[:widest] + [(index_at[widest] + 1) % values.shape[widest]] + index_at[widest + 1:]
    return values.at[tuple(index_at)].set(least).at[tuple(neighbour)].set(largest)


def block_levels(key, dims, pieces, least, high):
    def one(position, shards_of):
        heights = jax.random.uniform(jax.random.fold_in(jax.random.fold_in(key, 6), position), (shards_of,), jnp.float32, least / len(pieces), high / len(pieces))
        return jnp.repeat(jnp.exp(heights), dims[position] // shards_of).reshape((-1,) + (1,) * (len(dims) - position - 1))

    gain = one(*pieces[0])
    for cut in pieces[1:]:
        gain = gain * one(*cut)
    return gain


def normal_values(rng, shape, scale, reach, shards=(), kind=jnp.bfloat16):
    values = scale * jax.random.normal(rng, shape, jnp.float32)
    if shards:
        values = values * block_levels(rng, shape, shards, -0.22, 0.18)
    return jnp.clip(values, -reach, reach).astype(kind)


def setup_inputs(seed: int = 0) -> dict:
    splits = jax.random.split(jax.random.key(seed), 21)
    return {
        "pixels": normal_values(splits[0], (BANDS, PIX, DATES, LOTS), 1.0, 6.0, ((2, 32), (3, 8))),
        "counts": touch_ends(jax.random.randint(splits[1], (DATES, LOTS), 1, PIX + 1), jax.random.fold_in(splits[1], 1), 1, PIX).astype(jnp.int32),
        "edge_pixels": jnp.clip(1.5 + 4.5 * jax.random.uniform(splits[2], (BANDS, EDGE, DATES, STR_TOTAL), jnp.float32) ** block_levels(splits[2], (BANDS, EDGE, DATES, STR_TOTAL), ((2, 32), (3, 8)), -0.2, 0.2), 1.5, 6.0).astype(jnp.bfloat16),
        "edge_mask": touch_ends((jax.random.randint(splits[3], (EDGE, DATES, STR_TOTAL), 0, 4) < 3).astype(jnp.int32), jax.random.fold_in(splits[3], 1), 0, 1),
        "straddle_lot": draw_straddle_lot(jax.random.fold_in(splits[20], 71), 0),
        "date_days": draw_date_days(jax.random.fold_in(splits[20], 71), 0),
        "w_first": normal_values(splits[6], (H1, BANDS), BANDS ** -0.5, 1.75),
        "b_first": normal_values(splits[7], (H1,), 0.5, 3.0, (), jnp.float32),
        "w_second": normal_values(splits[8], (PFEAT, H1), H1 ** -0.5, 1.0),
        "b_second": normal_values(splits[9], (PFEAT,), 0.5, 3.0, (), jnp.float32),
        "w_pool": normal_values(splits[10], (2 * PFEAT, EMB), (2 * PFEAT) ** -0.5, 0.375),
        "b_pool": normal_values(splits[11], (EMB,), 0.5, 3.0, (), jnp.float32),
        "ln_one": jnp.clip(1.0 + 0.1 * jax.random.normal(splits[12], (EMB,), jnp.float32), 0.5, 1.5),
        "w_query": draw_w_query(jax.random.fold_in(splits[20], 71), 0),
        "w_key": draw_w_key(jax.random.fold_in(splits[20], 71), 0),
        "w_value": normal_values(splits[15], (EMB, EMB), EMB ** -0.5, 0.5),
        "w_out": normal_values(splits[16], (EMB, EMB), EMB ** -0.5, 0.5),
        "ln_two": jnp.clip(1.0 + 0.1 * jax.random.normal(splits[17], (EMB,), jnp.float32), 0.5, 1.5),
        "w_up": normal_values(splits[18], (EMB, FFN), EMB ** -0.5, 0.5),
        "w_down": normal_values(splits[19], (FFN, EMB), FFN ** -0.5, 0.25),
    }


VAR_FLOOR = 0.05
NORM_EPS = 1e-05

def pixel_stats(patch, usable, w_first, b_first, w_second, b_second):
    band_count, slot_count, columns = patch.shape
    flattened = patch.reshape(band_count, slot_count * columns)
    h_one = jnp.maximum(jnp.dot(w_first, flattened, preferred_element_type=jnp.float32) + b_first[:, None], 0.0).astype(jnp.bfloat16)
    h_two = jnp.maximum(jnp.dot(w_second, h_one, preferred_element_type=jnp.float32) + b_second[:, None], 0.0)
    h_two = h_two.reshape(h_two.shape[0], slot_count, columns)
    weighted = h_two * usable[None]
    return (lax.optimization_barrier(jnp.sum(weighted, axis=1)), lax.optimization_barrier(jnp.sum(weighted * h_two, axis=1)), lax.optimization_barrier(jnp.sum(usable, axis=0)))

def pool_stats(sum_all, square_all, count_all):
    average = sum_all / count_all
    spread = jnp.sqrt(jnp.maximum(square_all / count_all - average * average, VAR_FLOOR))
    return jnp.concatenate([average, spread], axis=-2).astype(jnp.bfloat16)

def position_code(day_numbers, model_width):
    half_ids = jnp.arange(model_width // 2, dtype=jnp.float32)
    freq_rate = jnp.exp(-(2.0 * half_ids / model_width) * math.log(1000.0))
    phase_angle = day_numbers.astype(jnp.float32)[:, None] * freq_rate[None]
    return jnp.stack([jnp.sin(phase_angle), jnp.cos(phase_angle)], axis=-1).reshape(day_numbers.shape[0], model_width)

def layer_norm(inputs, scale_gain):
    average = lax.optimization_barrier(jnp.mean(inputs, axis=-1, keepdims=True))
    centered = inputs - average
    variance = lax.optimization_barrier(jnp.mean(centered * centered, axis=-1, keepdims=True))
    return centered * lax.rsqrt(variance + NORM_EPS) * scale_gain

def temporal_layer(series, params):
    ln_one, w_query, w_key, w_value, w_out, ln_two, w_up, w_down = params
    length, model_width = series.shape
    head_width = model_width // HEADS
    carried = series.astype(jnp.float32)
    normed = layer_norm(carried, ln_one).astype(jnp.bfloat16)
    queries = jnp.dot(normed, w_query, preferred_element_type=jnp.float32).astype(jnp.bfloat16).reshape(length, HEADS, head_width)
    key_rows = jnp.dot(normed, w_key, preferred_element_type=jnp.float32).astype(jnp.bfloat16).reshape(length, HEADS, head_width)
    values = jnp.dot(normed, w_value, preferred_element_type=jnp.float32).astype(jnp.bfloat16).reshape(length, HEADS, head_width)
    scores = jnp.einsum('qhd,khd->hqk', queries.astype(jnp.float32), key_rows.astype(jnp.float32)) / math.sqrt(head_width)
    att_weights = jax.nn.softmax(scores, axis=-1).astype(jnp.bfloat16)
    mixture = jnp.einsum('hqk,khd->qhd', att_weights.astype(jnp.float32), values.astype(jnp.float32))
    mixture = mixture.reshape(length, model_width).astype(jnp.bfloat16)
    carried = carried + jnp.dot(mixture, w_out, preferred_element_type=jnp.float32)
    normed_two = layer_norm(carried, ln_two).astype(jnp.bfloat16)
    hidden = jax.nn.gelu(jnp.dot(normed_two, w_up, preferred_element_type=jnp.float32), approximate=False).astype(jnp.bfloat16)
    return (carried + jnp.dot(hidden, w_down, preferred_element_type=jnp.float32)).astype(jnp.bfloat16)

def reference(pixels, counts, edge_pixels, edge_mask, straddle_lot, date_days, w_first, b_first, w_second, b_second, w_pool, b_pool, ln_one, w_query, w_key, w_value, w_out, ln_two, w_up, w_down):
    day_code = position_code(date_days, EMB)
    owner_lot = jnp.arange(STR_TOTAL, dtype=jnp.int32) // STR_G * LOTS_G + straddle_lot.astype(jnp.int32)
    slot_ids = jnp.arange(PIX, dtype=jnp.int32)

    def per_date(date_index):
        patch = lax.dynamic_index_in_dim(pixels, date_index, 2, keepdims=False)
        filled = lax.dynamic_index_in_dim(counts, date_index, 0, keepdims=False)
        usable = (slot_ids[:, None] < filled[None, :]).astype(jnp.float32)
        sum_all, square_all, count_all = pixel_stats(patch, usable, w_first, b_first, w_second, b_second)
        edge_patch = lax.dynamic_index_in_dim(edge_pixels, date_index, 2, keepdims=False)
        edge_usable = lax.dynamic_index_in_dim(edge_mask, date_index, 1, keepdims=False).astype(jnp.float32)
        edge_sum, edge_square, edge_count = pixel_stats(edge_patch, edge_usable, w_first, b_first, w_second, b_second)
        edge_sum = jnp.roll(edge_sum, STR_G, axis=1)
        edge_square = jnp.roll(edge_square, STR_G, axis=1)
        edge_count = jnp.roll(edge_count, STR_G, axis=0)
        sum_all = sum_all.at[:, owner_lot].add(edge_sum)
        square_all = square_all.at[:, owner_lot].add(edge_square)
        count_all = count_all.at[owner_lot].add(edge_count)
        pooled = pool_stats(sum_all, square_all, count_all[None])
        embedded = jnp.dot(pooled.T, w_pool, preferred_element_type=jnp.float32) + b_pool[None] + day_code[date_index][None]
        return embedded.astype(jnp.bfloat16)
    embedded = lax.map(per_date, jnp.arange(DATES, dtype=jnp.int32))
    params = (ln_one, w_query, w_key, w_value, w_out, ln_two, w_up, w_down)
    lot_blocks = embedded.reshape(DATES, LOTS // 16, 16, EMB).transpose(1, 2, 0, 3)

    def per_block(lot_block):
        return jax.vmap(lambda series: temporal_layer(series, params))(lot_block)
    result = lax.map(per_block, lot_blocks)
    return result.transpose(2, 0, 1, 3).reshape(DATES, LOTS, EMB)
```

```python
import functools
import math

import jax
import jax.numpy as jnp
from jax import lax
from jax.experimental import pallas as pl
from jax.experimental.pallas import tpu as pltpu
from jax.sharding import PartitionSpec as P

HEADS = 4
VAR_FLOOR = 0.05
NORM_EPS = 1e-05
F32 = jnp.float32
BF16 = jnp.bfloat16
LANES = 128


def three_parts(values):
    high = lax.reduce_precision(values, 8, 7)
    rest = values - high
    middle = lax.reduce_precision(rest, 8, 7)
    low = rest - middle
    return high.astype(BF16), middle.astype(BF16), low.astype(BF16)


def pixel_weights(w_first, b_first, w_second, b_second, dates):
    h1, bands = w_first.shape
    feats = w_second.shape[0]
    same = jnp.eye(dates, dtype=BF16)
    first = (w_first.T[:, None, None, :] * same[None, :, :, None]).reshape(bands * dates, dates * h1)
    bias = jnp.stack(three_parts(b_first))
    bias = (bias[:, None, None, :] * same[None, :, :, None]).reshape(3 * dates, dates * h1)
    first = jnp.concatenate([first, bias], axis=0)
    pairs = dates // 2
    place = jnp.arange(pairs)
    dates_in = jnp.arange(4)
    dates_out = jnp.arange(2)
    hit = (dates_in[None, :, None] == (2 * (place % 2))[:, None, None] + dates_out[None, None, :]).astype(BF16)
    second = (hit[:, :, None, :, None] * w_second.T[None, None, :, None, :]).reshape(pairs, 4 * h1, 2 * feats)
    bias = jnp.stack(three_parts(b_second))
    absolute = (jnp.arange(dates)[None, :, None] == 2 * place[:, None, None] + dates_out[None, None, :]).astype(BF16)
    tail = (absolute[:, None, :, :, None] * bias[None, :, None, None, :]).reshape(pairs, 3 * dates, 2 * feats)
    gap = jnp.zeros((pairs, LANES - 3 * dates, 2 * feats), BF16)
    return first, jnp.concatenate([second, gap, tail], axis=1)


def relu_bf16(values):
    return jnp.maximum(values, 0.0).astype(BF16)


def pixel_kernel(
    pix_ref, cnt_ref, edge_ref, lot_ref, w1_ref, w2_ref, wp_ref, code_ref, perm_ref, out_ref,
    xt_ref, h_ref, es_ref, ec_ref, init_ref, inv_ref, pool_ref, e_ref,
):
    bands, slots, dates, lots = pix_ref.shape
    edge_slots = edge_ref.shape[1]
    pairs = w2_ref.shape[0]
    block = pl.program_id(0)
    rows = lots // 4

    def one_slot(p, source, mask, count):
        x = jnp.concatenate([source(b) for b in range(bands)] + [mask] * 3, axis=0)
        xt = x.T
        for r in range(4):
            xt_ref[r, pl.ds(p * rows, rows), :] = xt[r * rows : (r + 1) * rows]

    def first_layer(count):
        for r in range(4):
            z = jnp.dot(xt_ref[r, : count * rows, :], w1_ref[...], preferred_element_type=F32)
            z = relu_bf16(z)
            for g in range(4):
                h_ref[g, r, : count * rows, :] = z[:, g * LANES : (g + 1) * LANES]

    def second_layer(j, r, count):
        a = jnp.concatenate(
            [h_ref[j // 2, r, : count * rows, :], xt_ref[r, : count * rows, LANES:]], axis=1
        )
        z = jnp.dot(a, w2_ref[j], preferred_element_type=F32)
        total = square = None
        for p in range(count):
            part = jnp.maximum(z[p * rows : (p + 1) * rows], 0.0)
            total = part if total is None else total + part
            square = part * part if square is None else square + part * part
        return total, square

    @pl.when(block == 0)
    def _():
        half = lots // 2
        ec = jnp.zeros((dates, lots), F32)
        for p in range(edge_slots):
            mask = edge_ref[bands, p]
            one_slot(p, lambda b: edge_ref[b, p], mask, edge_slots)
            ec = ec + mask.astype(F32)
        ec_ref[...] = ec.astype(BF16)
        first_layer(edge_slots)
        es_ref[...] = jnp.zeros_like(es_ref)

        @pl.loop(0, pairs)
        def _(j):
            stats = [second_layer(j, r, edge_slots) for r in range(4)]
            for k in range(2):
                for r in range(2):
                    v = stats[r][k] + stats[r + 2][k]
                    for part in range(3):
                        cut = v.astype(BF16)
                        es_ref[j, pl.ds(part * half + r * rows, rows), 256 * k : 256 * (k + 1)] = cut
                        v = v - cut.astype(F32)

    counts = cnt_ref[...]
    for p in range(slots):
        mask = jnp.where(counts > p, 1.0, 0.0).astype(BF16)
        one_slot(p, lambda b: pix_ref[b, p] * mask, mask, slots)
    first_layer(slots)

    lot = lot_ref[...]
    lot_ids = lax.broadcasted_iota(jnp.int32, (lots, 256), 0) + block * lots
    chosen = jnp.where(lot_ids == lot, 1.0, 0.0).astype(BF16)
    lot_rows = lax.broadcasted_iota(jnp.int32, (lots, lots), 0) + block * lots
    chosen_twice = jnp.where(lot_rows == lot[:, :lots], 1.0, 0.0).astype(BF16)
    extra = lax.dot_general(ec_ref[...], chosen_twice, (((1,), (1,)), ((), ())), preferred_element_type=F32)
    inverse = 1.0 / (counts.astype(F32) + extra)
    inv_t = inverse.T
    for d in range(dates):
        inv_ref[d] = jnp.broadcast_to(inv_t[:, d : d + 1], (lots, LANES))

    @pl.loop(0, pairs)
    def _(j):
        init_ref[...] = jnp.dot(chosen, es_ref[j], preferred_element_type=F32)
        for r in range(4):
            total, square = second_layer(j, r, slots)
            here = slice(r * rows, (r + 1) * rows)
            total = total + init_ref[here, :256]
            square = square + init_ref[here, 256:]
            for k in range(2):
                inv = inv_ref[2 * j + k, here, :]
                lanes = slice(k * LANES, (k + 1) * LANES)
                average = total[:, lanes] * inv
                spread = jnp.maximum(square[:, lanes] * inv - average * average, VAR_FLOOR)
                spread = spread * lax.rsqrt(spread)
                pool_ref[2 * j + k, here, :LANES] = average.astype(BF16)
                pool_ref[2 * j + k, here, LANES:] = spread.astype(BF16)

    for d in range(dates):
        e = jnp.dot(pool_ref[d], wp_ref[...], preferred_element_type=F32) + code_ref[d : d + 1, :]
        e_ref[d] = e.astype(BF16)
    own = out_ref.shape[1]
    for k in range(0, lots // own, 2):
        both = jnp.concatenate(
            [e_ref[:, (k + s) * own : (k + s + 1) * own, :].reshape(dates * own, LANES) for s in range(2)], axis=1
        )
        y = jnp.dot(perm_ref[...], both, preferred_element_type=F32).astype(BF16)
        for s in range(2):
            out_ref[k + s] = y[:, s * LANES : (s + 1) * LANES].reshape(own, dates, LANES)


def pool_lots(pixels, counts, edges, lots_owned, w1, w2, w_pool, code, perm, peers):
    bands, slots, dates, lots = pixels.shape
    own = lots // peers
    block = LANES
    feats = w_pool.shape[1]
    pairs = dates // 2
    whole = lambda shape: pl.BlockSpec(shape, lambda i: (0,) * len(shape), pipeline_mode=pl.Buffered(1))
    return pl.pallas_call(
        pixel_kernel,
        grid=(lots // block,),
        in_specs=[
            pl.BlockSpec((bands, slots, dates, block), lambda i: (0, 0, 0, i)),
            pl.BlockSpec((dates, block), lambda i: (0, i)),
            whole(edges.shape),
            whole(lots_owned.shape),
            whole(w1.shape),
            whole(w2.shape),
            whole(w_pool.shape),
            whole(code.shape),
            whole(perm.shape),
        ],
        out_specs=pl.BlockSpec((block // own, own, dates, feats), lambda i: (i, 0, 0, 0)),
        out_shape=jax.ShapeDtypeStruct((peers, own, dates, feats), BF16),
        scratch_shapes=[
            pltpu.VMEM((4, slots * block // 4, 256), BF16),
            pltpu.VMEM((4, 4, slots * block // 4, LANES), BF16),
            pltpu.VMEM((pairs, 256, 512), BF16),
            pltpu.VMEM((dates, block), BF16),
            pltpu.VMEM((block, 512), F32),
            pltpu.VMEM((dates, block, LANES), F32),
            pltpu.VMEM((dates, block, 256), BF16),
            pltpu.VMEM((dates, block, LANES), BF16),
        ],
        compiler_params=pltpu.CompilerParams(vmem_limit_bytes=48 << 20),
        name="pixel_pool",
    )(pixels, counts, edges, lots_owned, w1, w2, w_pool, code, perm)


def erf_gelu(x):
    return 0.5 * x * (1.0 + lax.erf(x * (1.0 / math.sqrt(2.0))))


def norm_rows(x, gain):
    average = jnp.mean(x, axis=-1, keepdims=True)
    centered = x - average
    variance = jnp.mean(centered * centered, axis=-1, keepdims=True)
    return centered * lax.rsqrt(variance + NORM_EPS) * gain


def attention_kernel(
    e_ref, ln1_ref, wqk_ref, wvt_ref, wo_ref, ln2_ref, up_ref, down_ref, perm_ref, out_ref, enc_ref
):
    peers, own, dates, width = e_ref.shape
    total = peers * dates
    head = width // HEADS
    lane = lax.broadcasted_iota(jnp.int32, (total, width), 1)
    scale = math.log2(math.e) / math.sqrt(head)

    @pl.loop(0, own)
    def _(lot):
        series = e_ref[:, lot].reshape(total, width).astype(F32)
        normed = norm_rows(series, ln1_ref[...]).astype(BF16)
        both = jnp.dot(normed, wqk_ref[...], preferred_element_type=F32).astype(BF16)
        queries = both[:, :width]
        keys = both[:, width:]
        values_t = lax.dot_general(
            wvt_ref[...], normed, (((1,), (1,)), ((), ())), preferred_element_type=F32
        ).astype(BF16)
        ones = jnp.ones((16, total), BF16)
        mixed = []
        for h in range(HEADS):
            mine = jnp.where(lane // head == h, queries, jnp.zeros_like(queries))
            scores = lax.dot_general(keys, mine, (((1,), (1,)), ((), ())), preferred_element_type=F32)
            top = jnp.max(scores, axis=0, keepdims=True) * scale
            weights = jnp.exp2(scores * scale - top).astype(BF16)
            lhs = jnp.concatenate([values_t[h * head : (h + 1) * head], ones], axis=0)
            mix = jnp.dot(lhs, weights, preferred_element_type=F32)
            mixed.append((mix[:head] * (1.0 / mix[head : head + 1])).astype(BF16))
        mixture = jnp.concatenate(mixed, axis=0).T
        carried = series + jnp.dot(mixture, wo_ref[...], preferred_element_type=F32)
        normed_two = norm_rows(carried, ln2_ref[...]).astype(BF16)
        hidden = erf_gelu(jnp.dot(normed_two, up_ref[...], preferred_element_type=F32)).astype(BF16)
        encoded = carried + jnp.dot(hidden, down_ref[...], preferred_element_type=F32)
        enc_ref[lot] = encoded.astype(BF16).reshape(peers, dates, width)

    for p in range(0, peers, 2):
        two = jnp.concatenate([enc_ref[:, p + s].reshape(own * dates, width) for s in range(2)], axis=1)
        y = jnp.dot(perm_ref[...], two, preferred_element_type=F32).astype(BF16)
        for s in range(2):
            out_ref[pl.ds((p + s) * dates, dates)] = y[:, s * width : (s + 1) * width].reshape(dates, own, width)


def attend(embedded, ln1, wqk, wvt, wo, ln2, up, down, perm):
    peers, own, dates, width = embedded.shape
    return pl.pallas_call(
        attention_kernel,
        out_shape=jax.ShapeDtypeStruct((peers * dates, own, width), BF16),
        scratch_shapes=[pltpu.VMEM((own, peers, dates, width), BF16)],
        compiler_params=pltpu.CompilerParams(vmem_limit_bytes=56 << 20),
        name="attend",
    )(embedded, ln1, wqk, wvt, wo, ln2, up, down, perm)


def position_code(day_numbers, model_width):
    half_ids = jnp.arange(model_width // 2, dtype=F32)
    freq_rate = jnp.exp(-(2.0 * half_ids / model_width) * math.log(1000.0))
    phase_angle = day_numbers.astype(F32)[:, None] * freq_rate[None]
    return jnp.stack([jnp.sin(phase_angle), jnp.cos(phase_angle)], axis=-1).reshape(
        day_numbers.shape[0], model_width
    )


def swap_rows(minor, major):
    row = lax.broadcasted_iota(jnp.int32, (minor * major, minor * major), 0)
    col = lax.broadcasted_iota(jnp.int32, (minor * major, minor * major), 1)
    return (col == (row % minor) * major + row // minor).astype(BF16)


def edge_rows(edge_pixels, edge_mask):
    half = edge_pixels.shape[1] // 2
    mask = edge_mask.astype(BF16)
    rows = jnp.concatenate([edge_pixels * mask[None], mask[None]], axis=0)
    return jnp.concatenate([rows[:, :half], rows[:, half:]], axis=-1)


def per_device(
    pixels, counts, edge_pixels, edge_mask, straddle_lot, date_days,
    w_first, b_first, w_second, b_second, w_pool, b_pool,
    ln_one, w_query, w_key, w_value, w_out, ln_two, w_up, w_down,
):
    groups = lax.axis_size("group")
    peers = lax.axis_size("date")
    dates = pixels.shape[2]
    width = w_pool.shape[1]
    edges = lax.ppermute(
        edge_rows(edge_pixels, edge_mask), "group", [(i, (i + 1) % groups) for i in range(groups)]
    )
    w1, w2 = pixel_weights(w_first, b_first, w_second, b_second, dates)
    own_days = lax.dynamic_slice_in_dim(date_days, lax.axis_index("date") * dates, dates)
    code = position_code(own_days, width) + b_pool
    perm = swap_rows(dates, pixels.shape[3] // peers)
    lots_owned = jnp.concatenate([straddle_lot] * 3 + [jnp.full_like(straddle_lot, -1)])[None]
    pooled = pool_lots(pixels, counts, edges, lots_owned, w1, w2, w_pool, code, perm, peers)
    series = lax.all_to_all(pooled, "date", split_axis=0, concat_axis=0, tiled=True)
    wqk = jnp.concatenate([w_query, w_key], axis=1)
    return attend(
        series, ln_one[None], wqk, w_value.T, w_out, ln_two[None], w_up, w_down, perm
    )


def solution(mesh):
    return jax.shard_map(
        per_device,
        mesh=mesh,
        in_specs=(
            P(None, None, "date", "group"),
            P("date", "group"),
            P(None, None, "date", "group"),
            P(None, "date", "group"),
            P("group"),
        )
        + (P(),) * 15,
        out_specs=P(None, ("group", "date"), None),
        check_vma=False,
    )
```

```python
import functools
import math

import jax
import jax.numpy as jnp
from jax import lax
from jax.experimental import pallas as pl
from jax.experimental.pallas import tpu as pltpu
from jax.sharding import PartitionSpec as P

HEADS = 4
VAR_FLOOR = 0.05
NORM_EPS = 1e-05
F32 = jnp.float32
BF16 = jnp.bfloat16
LANES = 128


def three_parts(values):
    high = lax.reduce_precision(values, 8, 7)
    rest = values - high
    middle = lax.reduce_precision(rest, 8, 7)
    low = rest - middle
    return high.astype(BF16), middle.astype(BF16), low.astype(BF16)


def pixel_weights(w_first, b_first, w_second, b_second, dates):
    first = jnp.tile(jnp.concatenate([w_first.T, jnp.stack(three_parts(b_first))], axis=0), (1, dates))
    second = jnp.tile(w_second.T, (4, 4))
    bias = jnp.tile(jnp.stack(three_parts(b_second)), (1, 4))
    return first, second, bias


def relu_bf16(values):
    return jnp.maximum(values, 0.0).astype(BF16)


def spread_weights(t1_ref, t2_ref, b2_ref, w1_ref, w2_ref):
    taps, wide = t1_ref.shape
    groups = w2_ref.shape[0]
    dates = 4 * groups
    zero = jnp.zeros((), BF16)
    row = lax.broadcasted_iota(jnp.int32, (dates, wide), 0)
    col = lax.broadcasted_iota(jnp.int32, (dates, wide), 1)
    keep = row == col // (wide // dates)
    for b in range(taps):
        line = jnp.broadcast_to(t1_ref[b : b + 1, :].astype(F32), (dates, wide))
        w1_ref[b * dates : (b + 1) * dates, :] = jnp.where(keep, line, 0.0).astype(BF16)
    row_two = lax.broadcasted_iota(jnp.int32, (LANES, wide), 0)
    col_two = lax.broadcasted_iota(jnp.int32, (LANES, wide), 1)
    body = jnp.where(row_two // 32 == col_two // LANES, t2_ref[...].astype(F32), 0.0).astype(BF16)
    for g in range(groups):
        w2_ref[g, :LANES, :] = body
        w2_ref[g, LANES : 256 - 3 * dates, :] = jnp.zeros((LANES - 3 * dates, wide), BF16)
        mine = row == 4 * g + col // LANES
        for part in range(3):
            line = jnp.broadcast_to(b2_ref[part : part + 1, :].astype(F32), (dates, wide))
            start = 256 - 3 * dates + part * dates
            w2_ref[g, start : start + dates, :] = jnp.where(mine, line, 0.0).astype(BF16)


def swap_rows(size):
    row = lax.broadcasted_iota(jnp.int32, (size * size, size * size), 0)
    col = lax.broadcasted_iota(jnp.int32, (size * size, size * size), 1)
    return jnp.where(col == (row % size) * size + row // size, 1.0, 0.0).astype(BF16)


def pixel_kernel(
    pix_ref, cnt_ref, edge_ref, lot_ref, t1_ref, t2_ref, b2_ref, wp_ref, code_ref, out_ref,
    w1_ref, w2_ref, xt_ref, h_ref, es_ref, ec_ref, init_ref, inv_ref, pool_ref, e_ref, perm_ref, *, chunk,
):
    bands, slots, dates, lots = pix_ref.shape
    edge_slots = edge_ref.shape[1]
    groups = w2_ref.shape[0]
    block = pl.program_id(0)
    part_lots = LANES
    rows = part_lots // 4

    def mine(values):
        return jnp.concatenate([values[k + 8 * chunk : k + 8 * chunk + 8] for k in range(0, LANES, 16)], axis=0)

    def first_layer(count):
        def finish(r, z):
            z = relu_bf16(z)
            for g in range(4):
                h_ref[g, r, : count * rows, :] = z[:, g * LANES : (g + 1) * LANES]

        before = None
        for r in range(4):
            z = jnp.dot(xt_ref[r, : count * rows, :], w1_ref[...], preferred_element_type=F32)
            if before is not None:
                finish(r - 1, before)
            before = z
        finish(3, before)

    def hidden_two(g, r, count):
        a = jnp.concatenate([h_ref[g, r, : count * rows, :], xt_ref[r, : count * rows, LANES:]], axis=1)
        return jnp.dot(a, w2_ref[g], preferred_element_type=F32)

    def add_slots(z, count, lanes):
        total = square = None
        for p in range(count):
            part = jnp.maximum(z[p * rows : (p + 1) * rows, lanes], 0.0)
            total = part if total is None else total + part
            square = part * part if square is None else square + part * part
        return total, square

    @pl.when(block == 0)
    def _():
        spread_weights(t1_ref, t2_ref, b2_ref, w1_ref, w2_ref)
        perm_ref[...] = swap_rows(dates)
        half = LANES // 2
        ec = jnp.zeros((dates, LANES), F32)
        for p in range(edge_slots):
            mask = edge_ref[bands, p]
            xt = jnp.concatenate([edge_ref[b, p] for b in range(bands)] + [mask] * 3, axis=0).T
            for r in range(4):
                xt_ref[r, p * rows : (p + 1) * rows, :] = xt[r * rows : (r + 1) * rows]
            ec = ec + mask.astype(F32)
        ec_ref[...] = ec.astype(BF16)
        first_layer(edge_slots)
        es_ref[:, 3 * half :, :] = jnp.zeros((es_ref.shape[0], half, es_ref.shape[2]), BF16)

        @pl.loop(0, groups)
        def _(g):
            zs = [hidden_two(g, r, edge_slots) for r in range(4)]
            for c in range(2):
                lanes = slice(256 * c, 256 * (c + 1))
                stats = [add_slots(zs[r], edge_slots, lanes) for r in range(4)]
                for k in range(2):
                    for r in range(2):
                        v = stats[r][k] + stats[r + 2][k]
                        for part in range(3):
                            cut = v.astype(BF16)
                            here = slice(part * half + r * rows, part * half + (r + 1) * rows)
                            es_ref[2 * g + c, here, 256 * k : 256 * (k + 1)] = cut
                            v = v - cut.astype(F32)

    counts = cnt_ref[...]
    for p in range(slots):
        mask = jnp.where(counts > p, 1.0, 0.0).astype(BF16)
        for side in range(2):
            lanes = slice(side * LANES, (side + 1) * LANES)
            m = mask[:, lanes]
            x = jnp.concatenate([pix_ref[b, p, :, lanes] * m for b in range(bands)] + [m] * 3, axis=0)
            xt = mine(x.astype(F32).T).astype(BF16)
            for r in range(2):
                xt_ref[2 * side + r, p * rows : (p + 1) * rows, :] = xt[r * rows : (r + 1) * rows]
    first_layer(slots)

    lot = lot_ref[...]
    row = lax.broadcasted_iota(jnp.int32, (part_lots, 256), 0)
    lot_ids = block * lots + (row // 8) * 16 + 8 * chunk + row % 8
    chosen = jnp.where(lot_ids == lot, 1.0, 0.0).astype(BF16)
    lot_rows = lax.broadcasted_iota(jnp.int32, (lots, LANES), 0) + block * lots
    chosen_twice = jnp.where(lot_rows == lot[:, :LANES], 1.0, 0.0).astype(BF16)
    extra = lax.dot_general(ec_ref[...], chosen_twice, (((1,), (1,)), ((), ())), preferred_element_type=F32)
    inverse = 1.0 / (counts.astype(F32) + extra)
    inv_t = jnp.concatenate([mine(inverse[:, s * LANES : (s + 1) * LANES].T) for s in range(2)], axis=0)
    for d in range(dates):
        inv_ref[d] = jnp.broadcast_to(inv_t[:, d : d + 1], (part_lots, LANES))

    @pl.loop(0, groups)
    def _(g):
        def finish(r, z):
            here = slice(r * rows, (r + 1) * rows)
            for c in range(2):
                total, square = add_slots(z, slots, slice(256 * c, 256 * (c + 1)))
                total = total + init_ref[c, here, :256]
                square = square + init_ref[c, here, 256:]
                for k in range(2):
                    d = 4 * g + 2 * c + k
                    inv = inv_ref[d, here, :]
                    lanes = slice(k * LANES, (k + 1) * LANES)
                    average = total[:, lanes] * inv
                    spread = jnp.maximum(square[:, lanes] * inv - average * average, VAR_FLOOR)
                    spread = spread * lax.rsqrt(spread)
                    pool_ref[d, here, :LANES] = average.astype(BF16)
                    pool_ref[d, here, LANES:] = spread.astype(BF16)

        for c in range(2):
            init_ref[c] = jnp.dot(chosen, es_ref[2 * g + c], preferred_element_type=F32)
        before = None
        for r in range(4):
            z = hidden_two(g, r, slots)
            if before is not None:
                finish(r - 1, before)
            before = z
        finish(3, before)

    e_all = jnp.dot(pool_ref[...].reshape(dates * part_lots, 256), wp_ref[...], preferred_element_type=F32)
    for d in range(dates):
        e_ref[d] = (e_all[d * part_lots : (d + 1) * part_lots] + code_ref[d : d + 1, :]).astype(BF16)
    for k in range(0, part_lots, 32):
        both = jnp.concatenate(
            [e_ref[:, k + s : k + s + 16, :].reshape(dates * 16, LANES) for s in (0, 16)], axis=1
        )
        y = jnp.dot(perm_ref[...], both, preferred_element_type=F32).astype(BF16)
        for s in range(2):
            out_ref[k // 8 + 2 * s : k // 8 + 2 * s + 2] = y[:, s * LANES : (s + 1) * LANES].reshape(2, 8, dates, LANES)


def pool_lots(pixels, counts, edges, lots_owned, taps, w_pool, code, peers, chunk):
    bands, slots, dates, lots = pixels.shape
    own = lots // peers // 2
    block = 2 * LANES
    feats = w_pool.shape[1]
    groups = dates // 4
    whole = lambda x: pl.BlockSpec(x.shape, lambda i: (0,) * x.ndim, pipeline_mode=pl.Buffered(1))
    fixed = (edges, lots_owned, *taps, w_pool, code)
    return pl.pallas_call(
        functools.partial(pixel_kernel, chunk=chunk),
        grid=(lots // block,),
        in_specs=[
            pl.BlockSpec((bands, slots, dates, block), lambda i: (0, 0, 0, i)),
            pl.BlockSpec((dates, block), lambda i: (0, i)),
        ]
        + [whole(x) for x in fixed],
        out_specs=pl.BlockSpec((LANES // own, own, dates, feats), lambda i: (i, 0, 0, 0)),
        out_shape=jax.ShapeDtypeStruct((peers, own, dates, feats), BF16),
        scratch_shapes=[
            pltpu.VMEM((256, 512), BF16),
            pltpu.VMEM((groups, 256, 512), BF16),
            pltpu.VMEM((4, slots * LANES // 4, 256), BF16),
            pltpu.VMEM((4, 4, slots * LANES // 4, LANES), BF16),
            pltpu.VMEM((2 * groups, 256, 512), BF16),
            pltpu.VMEM((dates, LANES), BF16),
            pltpu.VMEM((2, LANES, 512), F32),
            pltpu.VMEM((dates, LANES, LANES), F32),
            pltpu.VMEM((dates, LANES, 256), BF16),
            pltpu.VMEM((dates, LANES, LANES), BF16),
            pltpu.VMEM((256, 256), BF16),
        ],
        compiler_params=pltpu.CompilerParams(vmem_limit_bytes=48 << 20),
        name=f"pixel_pool_{chunk}",
    )(pixels, counts, *fixed)


def erf_gelu(x):
    return 0.5 * x * (1.0 + lax.erf(x * (1.0 / math.sqrt(2.0))))


def norm_rows(x, gain):
    average = jnp.mean(x, axis=-1, keepdims=True)
    centered = x - average
    variance = jnp.mean(centered * centered, axis=-1, keepdims=True)
    return centered * lax.rsqrt(variance + NORM_EPS) * gain


def attention_kernel(
    e_ref, ln1_ref, wqv_ref, wkt_ref, wo_ref, ln2_ref, up_ref, down_ref, *rest, last,
):
    if last:
        first_ref, out_ref, enc_ref, q_ref, v_ref, k_ref, mix_ref = rest
    else:
        enc_ref, q_ref, v_ref, k_ref, mix_ref = rest
    peers, own, dates, width = e_ref.shape
    total = peers * dates
    head = width // HEADS
    together = q_ref.shape[0]
    tall = 256
    scale = math.log2(math.e) / math.sqrt(head)

    def rows_of(lot):
        return jnp.concatenate([e_ref[:, lot + l].reshape(total, width) for l in range(together)], axis=0).astype(F32)

    def project(lot):
        normed = norm_rows(rows_of(lot), ln1_ref[...]).astype(BF16)
        both = jnp.dot(normed, wqv_ref[...], preferred_element_type=F32).astype(BF16)
        keys_t = lax.dot_general(
            wkt_ref[...], normed, (((1,), (1,)), ((), ())), preferred_element_type=F32
        ).astype(BF16)
        for l in range(together):
            here = slice(l * total, (l + 1) * total)
            q_ref[l] = both[here, :width]
            v_ref[l] = both[here, width:]
            k_ref[l] = keys_t[:, here]

    def mix_dates(l):
        lane = lax.broadcasted_iota(jnp.int32, (total, width), 1)
        ones = jnp.ones((total, width), BF16)
        zero = jnp.zeros((total, width), BF16)
        parts = [None] * (total // tall)
        for h in range(HEADS):
            mine = lane // head == h
            queries = jnp.where(mine, q_ref[l], zero)
            values = jnp.concatenate([jnp.where(mine, v_ref[l], zero), ones], axis=1)
            for b in range(total // tall):
                here = slice(b * tall, (b + 1) * tall)
                scores = jnp.dot(queries[here], k_ref[l], preferred_element_type=F32)
                top = jnp.max(scores, axis=1, keepdims=True) * scale
                weights = jnp.exp2(scores * scale - top).astype(BF16)
                mix = jnp.dot(weights, values, preferred_element_type=F32)
                mix = mix[:, :width] * (1.0 / mix[:, width:])
                parts[b] = mix if parts[b] is None else parts[b] + mix
        mix_ref[l] = jnp.concatenate(parts, axis=0).astype(BF16)

    def feed_forward(lot):
        mixture = mix_ref[...].reshape(together * total, width)
        carried = rows_of(lot) + jnp.dot(mixture, wo_ref[...], preferred_element_type=F32)
        normed_two = norm_rows(carried, ln2_ref[...]).astype(BF16)
        hidden = erf_gelu(jnp.dot(normed_two, up_ref[...], preferred_element_type=F32)).astype(BF16)
        encoded = (carried + jnp.dot(hidden, down_ref[...], preferred_element_type=F32)).astype(BF16)
        for l in range(together):
            enc_ref[lot + l] = encoded[l * total : (l + 1) * total].reshape(peers, dates, width)

    @pl.loop(0, own, step=together)
    def _(lot):
        project(lot)

        @pl.loop(0, together, step=2)
        def _(l):
            mix_dates(l)
            mix_dates(l + 1)

        feed_forward(lot)

    if last:
        perm = swap_rows(dates)
        for p in range(0, peers, 2):
            two = jnp.concatenate(
                [
                    jnp.concatenate([first_ref[:, p + s], enc_ref[:, p + s]], axis=0).reshape(2 * own * dates, width)
                    for s in range(2)
                ],
                axis=1,
            )
            y = jnp.dot(perm, two, preferred_element_type=F32).astype(BF16)
            for s in range(2):
                here = slice((p + s) * dates, (p + s + 1) * dates)
                out_ref[here] = y[:, s * width : (s + 1) * width].reshape(dates, 2 * own, width)


def attend(embedded, params, first=None):
    peers, own, dates, width = embedded.shape
    total = peers * dates
    together = 4
    scratch = [
        pltpu.VMEM((together, total, width), BF16),
        pltpu.VMEM((together, total, width), BF16),
        pltpu.VMEM((together, width, total), BF16),
        pltpu.VMEM((together, total, width), BF16),
    ]
    last = first is not None
    mid = (own, peers, dates, width)
    return pl.pallas_call(
        functools.partial(attention_kernel, last=last),
        out_shape=jax.ShapeDtypeStruct((total, 2 * own, width) if last else mid, BF16),
        scratch_shapes=([pltpu.VMEM(mid, BF16)] if last else []) + scratch,
        compiler_params=pltpu.CompilerParams(vmem_limit_bytes=48 << 20),
        name="attend_last" if last else "attend_first",
    )(embedded, *params, *([first] if last else []))


def position_code(day_numbers, model_width):
    half_ids = jnp.arange(model_width // 2, dtype=F32)
    freq_rate = jnp.exp(-(2.0 * half_ids / model_width) * math.log(1000.0))
    phase_angle = day_numbers.astype(F32)[:, None] * freq_rate[None]
    return jnp.stack([jnp.sin(phase_angle), jnp.cos(phase_angle)], axis=-1).reshape(
        day_numbers.shape[0], model_width
    )


def edge_kernel(pix_ref, mask_ref, out_ref):
    bands, slots = pix_ref.shape[:2]
    half = slots // 2
    for p in range(half):
        masks = [jnp.where(mask_ref[p + s * half] > 0, 1.0, 0.0) for s in range(2)]
        out_ref[bands, p] = jnp.concatenate(masks, axis=-1).astype(BF16)
        for b in range(bands):
            two = [pix_ref[b, p + s * half].astype(F32) * masks[s] for s in range(2)]
            out_ref[b, p] = jnp.concatenate(two, axis=-1).astype(BF16)


def edge_rows(edge_pixels, edge_mask):
    bands, slots, dates, blocks = edge_pixels.shape
    return pl.pallas_call(
        edge_kernel,
        out_shape=jax.ShapeDtypeStruct((bands + 1, slots // 2, dates, 2 * blocks), BF16),
        name="edge_rows",
    )(edge_pixels, edge_mask)


def per_device(
    pixels, counts, edge_pixels, edge_mask, straddle_lot, date_days,
    w_first, b_first, w_second, b_second, w_pool, b_pool,
    ln_one, w_query, w_key, w_value, w_out, ln_two, w_up, w_down,
):
    groups = lax.axis_size("group")
    peers = lax.axis_size("date")
    dates = pixels.shape[2]
    width = w_pool.shape[1]
    edges = lax.ppermute(
        edge_rows(edge_pixels, edge_mask), "group", [(i, (i + 1) % groups) for i in range(groups)]
    )
    taps = pixel_weights(w_first, b_first, w_second, b_second, dates)
    own_days = lax.dynamic_slice_in_dim(date_days, lax.axis_index("date") * dates, dates)
    code = position_code(own_days, width) + b_pool
    lots_owned = jnp.concatenate([straddle_lot] * 3 + [jnp.full_like(straddle_lot, -1)])[None]
    params = (
        ln_one[None], jnp.concatenate([w_query, w_value], axis=1), w_key.T, w_out, ln_two[None], w_up, w_down
    )
    series = []
    for chunk in range(2):
        pooled = pool_lots(pixels, counts, edges, lots_owned, taps, w_pool, code, peers, chunk)
        series.append(lax.all_to_all(pooled, "date", split_axis=0, concat_axis=0, tiled=True))
    return attend(series[1], params, attend(series[0], params))


def solution(mesh):
    return jax.shard_map(
        per_device,
        mesh=mesh,
        in_specs=(
            P(None, None, "date", "group"),
            P("date", "group"),
            P(None, None, "date", "group"),
            P(None, "date", "group"),
            P("group"),
        )
        + (P(),) * 15,
        out_specs=P(None, ("group", "date"), None),
        check_vma=False,
    )
```

```python
import functools
import math

import jax
import jax.numpy as jnp
from jax import lax
from jax.experimental import pallas as pl
from jax.experimental.pallas import tpu as pltpu
from jax.sharding import PartitionSpec as P

HEADS = 4
VAR_FLOOR = 0.05
NORM_EPS = 1e-05
F32 = jnp.float32
BF16 = jnp.bfloat16
LANES = 128


def relu_bf16(values):
    return jnp.maximum(values, 0.0).astype(BF16)


NT = (((1,), (1,)), ((), ()))


def ones_where(condition):
    return jnp.where(condition, 1.0, 0.0).astype(BF16)


def grid_of(shape):
    return lax.broadcasted_iota(jnp.int32, shape, 0), lax.broadcasted_iota(jnp.int32, shape, 1)


def three_parts(values):
    parts = []
    for _ in range(3):
        parts.append(values.astype(BF16))
        values = values - parts[-1].astype(F32)
    return parts


def spread_weights(wf_ref, bf_ref, ws_ref, bs_ref, w1_ref, w2_ref):
    h1, bands = wf_ref.shape
    feats = ws_ref.shape[0]
    groups = w2_ref.shape[0]
    dates = 4 * groups
    wide = dates * h1
    row, col = grid_of((h1, wide))
    repeat = ones_where(row == col % h1)
    row, col = grid_of((16, bands))
    turned = lax.dot_general(ones_where(row == col), wf_ref[...], NT, preferred_element_type=F32).astype(BF16)
    taps = jnp.dot(turned, repeat, preferred_element_type=F32)
    row, col = grid_of((dates, wide))
    keep = row == col // h1
    for b in range(bands):
        line = jnp.broadcast_to(taps[b : b + 1], (dates, wide))
        w1_ref[b * dates : (b + 1) * dates, :] = jnp.where(keep, line, 0.0).astype(BF16)
    for part, values in enumerate(three_parts(jnp.broadcast_to(bf_ref[...], (dates, h1)))):
        line = jnp.dot(values, repeat, preferred_element_type=F32)
        start = (bands + part) * dates
        w1_ref[start : start + dates, :] = jnp.where(keep, line, 0.0).astype(BF16)
    row, col = grid_of((4 * h1, h1))
    stacked = lax.dot_general(ones_where(row % h1 == col), ws_ref[...], NT, preferred_element_type=F32)
    row_two, col_two = grid_of((4 * h1, 4 * feats))
    body = jnp.where(row_two // h1 == col_two // feats, jnp.concatenate([stacked] * 4, axis=1), 0.0).astype(BF16)
    lines = [part.astype(F32) for part in three_parts(jnp.broadcast_to(bs_ref[...], (dates, feats)))]
    lines = [jnp.concatenate([line] * 4, axis=1) for line in lines]
    row, col = grid_of((dates, 4 * feats))
    gap = 256 - 3 * dates
    for g in range(groups):
        w2_ref[g, : 4 * h1, :] = body
        w2_ref[g, 4 * h1 : gap, :] = jnp.zeros((gap - 4 * h1, 4 * feats), BF16)
        for part in range(3):
            start = gap + part * dates
            w2_ref[g, start : start + dates, :] = jnp.where(row == 4 * g + col // feats, lines[part], 0.0).astype(BF16)


def swap_rows(size):
    row = lax.broadcasted_iota(jnp.int32, (size * size, size * size), 0)
    col = lax.broadcasted_iota(jnp.int32, (size * size, size * size), 1)
    return jnp.where(col == (row % size) * size + row // size, 1.0, 0.0).astype(BF16)


ROWS = 32


def first_layer(xt, h_ref, w1_ref, count):
    def finish(r, z):
        z = relu_bf16(z)
        for g in range(4):
            h_ref[g, r, : count * ROWS, :] = z[:, g * LANES : (g + 1) * LANES]

    before = None
    for r in range(4):
        z = jnp.dot(xt(r), w1_ref[...], preferred_element_type=F32)
        if before is not None:
            finish(r - 1, before)
        before = z
    finish(3, before)


def second_layer(xt, h_ref, w2_ref, g, r, count):
    a = jnp.concatenate([h_ref[g, r, : count * ROWS, :], xt(r)[:, LANES:]], axis=1)
    return jnp.dot(a, w2_ref[g], preferred_element_type=F32)


def add_slots(z, count, lanes):
    total = square = None
    for p in range(count):
        part = jnp.maximum(z[p * ROWS : (p + 1) * ROWS, lanes], 0.0)
        total = part if total is None else total + part
        square = part * part if square is None else square + part * part
    return total, square


def halves(values):
    return [
        jnp.concatenate([values[k + 8 * c : k + 8 * c + 8] for k in range(0, LANES, 16)], axis=0) for c in range(2)
    ]


def sums_of(xt, h_ref, w1_ref, w2_ref, out_ref, slots):
    first_layer(xt, h_ref, w1_ref, slots)

    @pl.loop(0, w2_ref.shape[0])
    def _(g):
        def finish(r, z):
            here = slice(r * ROWS, (r + 1) * ROWS)
            for c in range(2):
                total, square = add_slots(z, slots, slice(256 * c, 256 * (c + 1)))
                out_ref[0, g, c, here, :256] = total
                out_ref[0, g, c, here, 256:] = square

        before = None
        for r in range(4):
            z = second_layer(xt, h_ref, w2_ref, g, r, slots)
            if before is not None:
                finish(r - 1, before)
            before = z
        finish(3, before)


def first_sums_kernel(
    pix_ref, cnt_ref, wf_ref, bf_ref, ws_ref, bs_ref, out_ref, other_ref, w1_ref, w2_ref, xt_ref, h_ref
):
    bands, slots = pix_ref.shape[:2]

    @pl.when(pl.program_id(0) == 0)
    def _():
        spread_weights(wf_ref, bf_ref, ws_ref, bs_ref, w1_ref, w2_ref)

    counts = cnt_ref[...]
    for p in range(slots):
        mask = ones_where(counts > p)
        for side in range(2):
            lanes = slice(side * LANES, (side + 1) * LANES)
            m = mask[:, lanes]
            x = jnp.concatenate([pix_ref[b, p, :, lanes] * m for b in range(bands)] + [m] * 3, axis=0)
            for c, xt in enumerate(halves(x.astype(F32).T)):
                xt = xt.astype(BF16)
                for r in range(2):
                    part = xt[r * ROWS : (r + 1) * ROWS]
                    if c == 0:
                        xt_ref[2 * side + r, p * ROWS : (p + 1) * ROWS, :] = part
                    else:
                        other_ref[0, 2 * side + r, p * ROWS : (p + 1) * ROWS, :] = part
    sums_of(lambda r: xt_ref[r], h_ref, w1_ref, w2_ref, out_ref, slots)


def second_sums_kernel(xt_ref, wf_ref, bf_ref, ws_ref, bs_ref, out_ref, w1_ref, w2_ref, h_ref):
    @pl.when(pl.program_id(0) == 0)
    def _():
        spread_weights(wf_ref, bf_ref, ws_ref, bs_ref, w1_ref, w2_ref)

    sums_of(lambda r: xt_ref[0, r], h_ref, w1_ref, w2_ref, out_ref, xt_ref.shape[2] // ROWS)


def edge_sums_kernel(edge_ref, wf_ref, bf_ref, ws_ref, bs_ref, es_ref, ec_ref, w1_ref, w2_ref, xt_ref, h_ref):
    bands = edge_ref.shape[0] - 1
    slots, dates = edge_ref.shape[1:3]
    half = LANES // 2
    spread_weights(wf_ref, bf_ref, ws_ref, bs_ref, w1_ref, w2_ref)
    ec = jnp.zeros((dates, LANES), F32)
    for p in range(slots):
        mask = edge_ref[bands, p]
        xt = jnp.concatenate([edge_ref[b, p] for b in range(bands)] + [mask] * 3, axis=0).T
        for r in range(4):
            xt_ref[r, p * ROWS : (p + 1) * ROWS, :] = xt[r * ROWS : (r + 1) * ROWS]
        ec = ec + mask.astype(F32)
    ec_ref[...] = ec.astype(BF16)
    first_layer(lambda r: xt_ref[r], h_ref, w1_ref, slots)
    es_ref[:, 3 * half :, :] = jnp.zeros((es_ref.shape[0], half, es_ref.shape[2]), BF16)

    @pl.loop(0, w2_ref.shape[0])
    def _(g):
        zs = [second_layer(lambda r: xt_ref[r], h_ref, w2_ref, g, r, slots) for r in range(4)]
        for c in range(2):
            lanes = slice(256 * c, 256 * (c + 1))
            stats = [add_slots(zs[r], slots, lanes) for r in range(4)]
            for k in range(2):
                for r in range(2):
                    v = stats[r][k] + stats[r + 2][k]
                    for part, cut in enumerate(three_parts(v)):
                        here = slice(part * half + r * ROWS, part * half + (r + 1) * ROWS)
                        es_ref[2 * g + c, here, 256 * k : 256 * (k + 1)] = cut


def pool_kernel(
    sums_ref, cnt_ref, es_ref, ec_ref, lot_ref, wp_ref, code_ref, out_ref,
    chosen_ref, inv_ref, pool_ref, e_ref, perm_ref, *, chunk,
):
    block, g = pl.program_id(0), pl.program_id(1)
    dates, lots = cnt_ref.shape

    @pl.when(g == 0)
    def _():
        perm_ref[...] = swap_rows(dates)
        lot = jnp.concatenate([lot_ref[...], lot_ref[...]], axis=1)
        lane = lax.broadcasted_iota(jnp.int32, lot.shape, 1)
        four = jnp.concatenate([lot, jnp.where(lane < LANES // 2, lot, -1)], axis=1)
        row = lax.broadcasted_iota(jnp.int32, (LANES, 256), 0)
        lot_ids = block * lots + (row // 8) * 16 + 8 * chunk + row % 8
        chosen_ref[...] = ones_where(lot_ids == four)
        lot_rows = lax.broadcasted_iota(jnp.int32, (lots, LANES), 0) + block * lots
        extra = lax.dot_general(ec_ref[...], ones_where(lot_rows == lot), NT, preferred_element_type=F32)
        inverse = 1.0 / (cnt_ref[...].astype(F32) + extra)
        inv_t = jnp.concatenate(
            [halves(inverse[:, s * LANES : (s + 1) * LANES].T)[chunk] for s in range(2)], axis=0
        )
        for d in range(dates):
            inv_ref[d] = jnp.broadcast_to(inv_t[:, d : d + 1], (LANES, LANES))

    for c in range(2):
        both = sums_ref[0, 0, c] + jnp.dot(chosen_ref[...], es_ref[c], preferred_element_type=F32)
        for k in range(2):
            d = 4 * g + 2 * c + k
            inv = inv_ref[d]
            average = both[:, k * LANES : (k + 1) * LANES] * inv
            spread = both[:, (2 + k) * LANES : (3 + k) * LANES] * inv - average * average
            spread = jnp.maximum(spread, VAR_FLOOR)
            spread = spread * lax.rsqrt(spread)
            pool_ref[d, :, :LANES] = average.astype(BF16)
            pool_ref[d, :, LANES:] = spread.astype(BF16)

    @pl.when(g == pl.num_programs(1) - 1)
    def _():
        e_all = jnp.dot(pool_ref[...].reshape(dates * LANES, 256), wp_ref[...], preferred_element_type=F32)
        for d in range(dates):
            e_ref[d] = (e_all[d * LANES : (d + 1) * LANES] + code_ref[d : d + 1, :]).astype(BF16)
        for k in range(0, LANES, 32):
            both = jnp.concatenate(
                [e_ref[:, k + s : k + s + 16, :].reshape(dates * 16, LANES) for s in (0, 16)], axis=1
            )
            y = jnp.dot(perm_ref[...], both, preferred_element_type=F32).astype(BF16)
            for s in range(2):
                here = slice(k // 8 + 2 * s, k // 8 + 2 * s + 2)
                out_ref[here] = y[:, s * LANES : (s + 1) * LANES].reshape(2, 8, dates, LANES)


def whole(x):
    return pl.BlockSpec(x.shape, lambda *_: (0,) * x.ndim, pipeline_mode=pl.Buffered(1))


def own_sums(weights, slots, dates, blocks, pixels=None, counts=None, turned=None):
    groups = dates // 4
    sums = jax.ShapeDtypeStruct((blocks, groups, 2, LANES, 512), F32)
    sums_spec = pl.BlockSpec((1,) + sums.shape[1:], lambda i: (i, 0, 0, 0, 0))
    tall = slots * ROWS
    laid = jax.ShapeDtypeStruct((blocks, 4, tall, 256), BF16)
    laid_spec = pl.BlockSpec((1,) + laid.shape[1:], lambda i: (i, 0, 0, 0))
    scratch = [pltpu.VMEM((256, 512), BF16), pltpu.VMEM((groups, 256, 512), BF16)]
    hidden = pltpu.VMEM((4, 4, tall, LANES), BF16)
    first = turned is None
    if first:
        bands = pixels.shape[0]
        inputs = (pixels, counts)
        specs = [
            pl.BlockSpec((bands, slots, dates, 256), lambda i: (0, 0, 0, i)),
            pl.BlockSpec((dates, 256), lambda i: (0, i)),
        ]
        scratch.append(pltpu.VMEM((4, tall, 256), BF16))
    else:
        inputs, specs = (turned,), [laid_spec]
    return pl.pallas_call(
        first_sums_kernel if first else second_sums_kernel,
        grid=(blocks,),
        in_specs=specs + [whole(x) for x in weights],
        out_specs=(sums_spec, laid_spec) if first else sums_spec,
        out_shape=(sums, laid) if first else sums,
        scratch_shapes=scratch + [hidden],
        compiler_params=pltpu.CompilerParams(vmem_limit_bytes=58 << 20),
        name="first_sums" if first else "second_sums",
    )(*inputs, *weights)


def edge_sums(edges, weights):
    _, slots, dates, lanes = edges.shape
    groups = dates // 4
    return pl.pallas_call(
        edge_sums_kernel,
        out_shape=(
            jax.ShapeDtypeStruct((2 * groups, 256, 512), BF16),
            jax.ShapeDtypeStruct((dates, lanes), BF16),
        ),
        scratch_shapes=[
            pltpu.VMEM((256, 512), BF16),
            pltpu.VMEM((groups, 256, 512), BF16),
            pltpu.VMEM((4, slots * ROWS, 256), BF16),
            pltpu.VMEM((4, 4, slots * ROWS, LANES), BF16),
        ],
        compiler_params=pltpu.CompilerParams(vmem_limit_bytes=58 << 20),
        name="edge_sums",
    )(edges, *weights)


def pool_lots(sums, counts, es, ec, lots_owned, w_pool, code, peers, chunk):
    blocks, groups = sums.shape[:2]
    dates = counts.shape[0]
    own = 8
    feats = w_pool.shape[1]
    fixed = (ec, lots_owned, w_pool, code)
    return pl.pallas_call(
        functools.partial(pool_kernel, chunk=chunk),
        grid=(blocks, groups),
        in_specs=[
            pl.BlockSpec((1, 1) + sums.shape[2:], lambda i, g: (i, g, 0, 0, 0)),
            pl.BlockSpec((dates, 256), lambda i, g: (0, i)),
            pl.BlockSpec((2,) + es.shape[1:], lambda i, g: (g, 0, 0)),
        ]
        + [whole(x) for x in fixed],
        out_specs=pl.BlockSpec((LANES // own, own, dates, feats), lambda i, g: (i, 0, 0, 0)),
        out_shape=jax.ShapeDtypeStruct((peers, own, dates, feats), BF16),
        scratch_shapes=[
            pltpu.VMEM((LANES, 256), BF16),
            pltpu.VMEM((dates, LANES, LANES), F32),
            pltpu.VMEM((dates, LANES, 256), BF16),
            pltpu.VMEM((dates, LANES, LANES), BF16),
            pltpu.VMEM((256, 256), BF16),
        ],
        compiler_params=pltpu.CompilerParams(vmem_limit_bytes=56 << 20),
        name=f"pool_{chunk}",
    )(sums, counts, es, *fixed)


def erf_gelu(x):
    return 0.5 * x * (1.0 + lax.erf(x * (1.0 / math.sqrt(2.0))))


def norm_rows(x, gain):
    average = jnp.mean(x, axis=-1, keepdims=True)
    centered = x - average
    variance = jnp.mean(centered * centered, axis=-1, keepdims=True)
    return centered * lax.rsqrt(variance + NORM_EPS) * gain


def attention_kernel(
    e_ref, ln1_ref, wq_ref, wk_ref, wv_ref, wo_ref, ln2_ref, up_ref, down_ref, *rest, last,
):
    if last:
        first_ref, out_ref, enc_ref, q_ref, v_ref, k_ref, mix_ref = rest
    else:
        enc_ref, q_ref, v_ref, k_ref, mix_ref = rest
    peers, own, dates, width = e_ref.shape
    total = peers * dates
    head = width // HEADS
    together = q_ref.shape[0]
    tall = 256
    scale = math.log2(math.e) / math.sqrt(head)

    def rows_of(lot):
        return jnp.concatenate([e_ref[:, lot + l].reshape(total, width) for l in range(together)], axis=0).astype(F32)

    def project(lot):
        normed = norm_rows(rows_of(lot), ln1_ref[...]).astype(BF16)
        weights = jnp.concatenate([wq_ref[...], wv_ref[...]], axis=1)
        both = jnp.dot(normed, weights, preferred_element_type=F32).astype(BF16)
        keys_t = lax.dot_general(wk_ref[...].T, normed, NT, preferred_element_type=F32).astype(BF16)
        for l in range(together):
            here = slice(l * total, (l + 1) * total)
            q_ref[l] = both[here, :width]
            v_ref[l] = both[here, width:]
            k_ref[l] = keys_t[:, here]

    def mix_dates(l):
        lane = lax.broadcasted_iota(jnp.int32, (total, width), 1)
        ones = jnp.ones((total, width), BF16)
        zero = jnp.zeros((total, width), BF16)
        parts = [None] * (total // tall)
        for h in range(HEADS):
            mine = lane // head == h
            queries = jnp.where(mine, q_ref[l], zero)
            values = jnp.concatenate([jnp.where(mine, v_ref[l], zero), ones], axis=1)
            for b in range(total // tall):
                here = slice(b * tall, (b + 1) * tall)
                scores = jnp.dot(queries[here], k_ref[l], preferred_element_type=F32)
                top = jnp.max(scores, axis=1, keepdims=True) * scale
                weights = jnp.exp2(scores * scale - top).astype(BF16)
                mix = jnp.dot(weights, values, preferred_element_type=F32)
                mix = mix[:, :width] * (1.0 / mix[:, width:])
                parts[b] = mix if parts[b] is None else parts[b] + mix
        mix_ref[l] = jnp.concatenate(parts, axis=0).astype(BF16)

    def feed_forward(lot):
        mixture = mix_ref[...].reshape(together * total, width)
        carried = rows_of(lot) + jnp.dot(mixture, wo_ref[...], preferred_element_type=F32)
        normed_two = norm_rows(carried, ln2_ref[...]).astype(BF16)
        hidden = erf_gelu(jnp.dot(normed_two, up_ref[...], preferred_element_type=F32)).astype(BF16)
        encoded = (carried + jnp.dot(hidden, down_ref[...], preferred_element_type=F32)).astype(BF16)
        for l in range(together):
            enc_ref[lot + l] = encoded[l * total : (l + 1) * total].reshape(peers, dates, width)

    @pl.loop(0, own, step=together)
    def _(lot):
        project(lot)

        @pl.loop(0, together, step=2)
        def _(l):
            mix_dates(l)
            mix_dates(l + 1)

        feed_forward(lot)

    if last:
        perm = swap_rows(dates)
        for p in range(0, peers, 2):
            two = jnp.concatenate(
                [
                    jnp.concatenate([first_ref[:, p + s], enc_ref[:, p + s]], axis=0).reshape(2 * own * dates, width)
                    for s in range(2)
                ],
                axis=1,
            )
            y = jnp.dot(perm, two, preferred_element_type=F32).astype(BF16)
            for s in range(2):
                here = slice((p + s) * dates, (p + s + 1) * dates)
                out_ref[here] = y[:, s * width : (s + 1) * width].reshape(dates, 2 * own, width)


def attend(embedded, params, first=None):
    peers, own, dates, width = embedded.shape
    total = peers * dates
    together = 4
    scratch = [
        pltpu.VMEM((together, total, width), BF16),
        pltpu.VMEM((together, total, width), BF16),
        pltpu.VMEM((together, width, total), BF16),
        pltpu.VMEM((together, total, width), BF16),
    ]
    last = first is not None
    mid = (own, peers, dates, width)
    return pl.pallas_call(
        functools.partial(attention_kernel, last=last),
        out_shape=jax.ShapeDtypeStruct((total, 2 * own, width) if last else mid, BF16),
        scratch_shapes=([pltpu.VMEM(mid, BF16)] if last else []) + scratch,
        compiler_params=pltpu.CompilerParams(vmem_limit_bytes=48 << 20),
        name="attend_last" if last else "attend_first",
    )(embedded, *params, *([first] if last else []))


def position_code(day_numbers, model_width):
    lane = lax.broadcasted_iota(jnp.int32, (day_numbers.shape[0], model_width), 1)
    freq_rate = jnp.exp(-(2.0 * (lane // 2).astype(F32) / model_width) * math.log(1000.0))
    phase_angle = day_numbers.astype(F32)[:, None] * freq_rate
    return jnp.where(lane % 2 == 0, jnp.sin(phase_angle), jnp.cos(phase_angle))


def edge_kernel(pix_ref, mask_ref, out_ref):
    bands, slots = pix_ref.shape[:2]
    half = slots // 2
    for p in range(half):
        masks = [jnp.where(mask_ref[p + s * half] > 0, 1.0, 0.0) for s in range(2)]
        out_ref[bands, p] = jnp.concatenate(masks, axis=-1).astype(BF16)
        for b in range(bands):
            two = [pix_ref[b, p + s * half].astype(F32) * masks[s] for s in range(2)]
            out_ref[b, p] = jnp.concatenate(two, axis=-1).astype(BF16)


def edge_rows(edge_pixels, edge_mask):
    bands, slots, dates, blocks = edge_pixels.shape
    return pl.pallas_call(
        edge_kernel,
        out_shape=jax.ShapeDtypeStruct((bands + 1, slots // 2, dates, 2 * blocks), BF16),
        name="edge_rows",
    )(edge_pixels, edge_mask)


def per_device(
    pixels, counts, edge_pixels, edge_mask, straddle_lot, date_days,
    w_first, b_first, w_second, b_second, w_pool, b_pool,
    ln_one, w_query, w_key, w_value, w_out, ln_two, w_up, w_down,
):
    groups = lax.axis_size("group")
    peers = lax.axis_size("date")
    dates = pixels.shape[2]
    width = w_pool.shape[1]
    edges = lax.ppermute(
        edge_rows(edge_pixels, edge_mask), "group", [(i, (i + 1) % groups) for i in range(groups)]
    )
    weights = (w_first, b_first[None], w_second, b_second[None])
    slots = pixels.shape[1]
    blocks = pixels.shape[3] // 256
    own_days = lax.dynamic_slice_in_dim(date_days, lax.axis_index("date") * dates, dates)
    code = position_code(own_days, width) + b_pool
    params = (ln_one[None], w_query, w_key, w_value, w_out, ln_two[None], w_up, w_down)
    sums, turned = own_sums(weights, slots, dates, blocks, pixels=pixels, counts=counts)
    es, ec = edge_sums(edges, weights)
    series = []
    for chunk in range(2):
        if chunk:
            sums = own_sums(weights, slots, dates, blocks, turned=turned)
        pooled = pool_lots(sums, counts, es, ec, straddle_lot[None], w_pool, code, peers, chunk)
        series.append(lax.all_to_all(pooled, "date", split_axis=0, concat_axis=0, tiled=True))
    return attend(series[1], params, attend(series[0], params))


def solution(mesh):
    return jax.shard_map(
        per_device,
        mesh=mesh,
        in_specs=(
            P(None, None, "date", "group"),
            P("date", "group"),
            P(None, None, "date", "group"),
            P(None, "date", "group"),
            P("group"),
        )
        + (P(),) * 15,
        out_specs=P(None, ("group", "date"), None),
        check_vma=False,
    )
```

```python
import functools
import math

import jax
import jax.numpy as jnp
from jax import lax
from jax.experimental import pallas as pl
from jax.experimental.pallas import tpu as pltpu
from jax.sharding import PartitionSpec as P

HEADS = 4
VAR_FLOOR = 0.05
NORM_EPS = 1e-05
F32 = jnp.float32
BF16 = jnp.bfloat16
LANES = 128


def relu_bf16(values):
    return jnp.maximum(values, 0.0).astype(BF16)


NT = (((1,), (1,)), ((), ()))


def ones_where(condition):
    return jnp.where(condition, 1.0, 0.0).astype(BF16)


def grid_of(shape):
    return lax.broadcasted_iota(jnp.int32, shape, 0), lax.broadcasted_iota(jnp.int32, shape, 1)


def three_parts(values):
    parts = []
    for _ in range(3):
        parts.append(values.astype(BF16))
        values = values - parts[-1].astype(F32)
    return parts


def spread_weights(wf_ref, bf_ref, ws_ref, bs_ref, w1_ref, w2_ref):
    bands, h1 = wf_ref.shape
    feats = ws_ref.shape[1]
    groups = w2_ref.shape[0]
    dates = 4 * groups
    wide = dates * h1
    row, col = grid_of((h1, wide))
    repeat = ones_where(row == col % h1)
    taps = jnp.dot(wf_ref[...], repeat, preferred_element_type=F32)
    row, col = grid_of((dates, wide))
    keep = row == col // h1
    for b in range(bands):
        line = jnp.broadcast_to(taps[b : b + 1], (dates, wide))
        w1_ref[b * dates : (b + 1) * dates, :] = jnp.where(keep, line, 0.0).astype(BF16)
    for part, values in enumerate(three_parts(jnp.broadcast_to(bf_ref[...], (dates, h1)))):
        line = jnp.dot(values, repeat, preferred_element_type=F32)
        start = (bands + part) * dates
        w1_ref[start : start + dates, :] = jnp.where(keep, line, 0.0).astype(BF16)
    stacked = jnp.concatenate([ws_ref[...].astype(F32)] * 4, axis=0)
    row_two, col_two = grid_of((4 * h1, 4 * feats))
    body = jnp.where(row_two // h1 == col_two // feats, jnp.concatenate([stacked] * 4, axis=1), 0.0).astype(BF16)
    lines = [part.astype(F32) for part in three_parts(jnp.broadcast_to(bs_ref[...], (dates, feats)))]
    lines = [jnp.concatenate([line] * 4, axis=1) for line in lines]
    row, col = grid_of((dates, 4 * feats))
    gap = 256 - 3 * dates
    for g in range(groups):
        w2_ref[g, : 4 * h1, :] = body
        w2_ref[g, 4 * h1 : gap, :] = jnp.zeros((gap - 4 * h1, 4 * feats), BF16)
        for part in range(3):
            start = gap + part * dates
            w2_ref[g, start : start + dates, :] = jnp.where(row == 4 * g + col // feats, lines[part], 0.0).astype(BF16)


def swap_rows(size):
    row = lax.broadcasted_iota(jnp.int32, (size * size, size * size), 0)
    col = lax.broadcasted_iota(jnp.int32, (size * size, size * size), 1)
    return jnp.where(col == (row % size) * size + row // size, 1.0, 0.0).astype(BF16)


ROWS = 32


def first_layer(xt, h_ref, w1_ref, count):
    def finish(r, z):
        z = relu_bf16(z)
        for g in range(4):
            h_ref[g, r, : count * ROWS, :] = z[:, g * LANES : (g + 1) * LANES]

    before = None
    for r in range(4):
        z = jnp.dot(xt(r), w1_ref[...], preferred_element_type=F32)
        if before is not None:
            finish(r - 1, before)
        before = z
    finish(3, before)


def second_layer(xt, h_ref, w2_ref, g, r, count):
    a = jnp.concatenate([h_ref[g, r, : count * ROWS, :], xt(r)[:, LANES:]], axis=1)
    return jnp.dot(a, w2_ref[g], preferred_element_type=F32)


def add_slots(z, count, lanes):
    total = square = None
    for p in range(count):
        part = jnp.maximum(z[p * ROWS : (p + 1) * ROWS, lanes], 0.0)
        total = part if total is None else total + part
        square = part * part if square is None else square + part * part
    return total, square


def halves(values):
    return [
        jnp.concatenate([values[k + 8 * c : k + 8 * c + 8] for k in range(0, LANES, 16)], axis=0) for c in range(2)
    ]


def lay_out_kernel(pix_ref, cnt_ref, first_ref, second_ref):
    bands, slots = pix_ref.shape[:2]
    counts = cnt_ref[...]
    for p in range(slots):
        mask = ones_where(counts > p)
        for side in range(2):
            lanes = slice(side * LANES, (side + 1) * LANES)
            m = mask[:, lanes]
            x = jnp.concatenate([pix_ref[b, p, :, lanes] * m for b in range(bands)] + [m] * 3, axis=0)
            for ref, xt in zip((first_ref, second_ref), halves(x.astype(F32).T)):
                xt = xt.astype(BF16)
                for r in range(2):
                    ref[0, 2 * side + r, p * ROWS : (p + 1) * ROWS, :] = xt[r * ROWS : (r + 1) * ROWS]


def pixel_kernel(
    xt_ref, cnt_ref, edge_ref, lot_ref, wf_ref, bf_ref, ws_ref, bs_ref, wp_ref, code_ref, out_ref,
    w1_ref, w2_ref, ext_ref, h_ref, es_ref, ec_ref, chosen_ref, init_ref, inv_ref, pool_ref, e_ref, perm_ref, *, chunk,
):
    block = pl.program_id(0)
    dates, lots = cnt_ref.shape
    slots = xt_ref.shape[2] // ROWS
    groups = w2_ref.shape[0]
    mine = lambda r: xt_ref[0, r]
    lot = jnp.concatenate([lot_ref[...], lot_ref[...]], axis=1)

    @pl.when(block == 0)
    def _():
        spread_weights(wf_ref, bf_ref, ws_ref, bs_ref, w1_ref, w2_ref)
        perm_ref[...] = swap_rows(dates)
        bands = edge_ref.shape[0] - 1
        edge_slots = edge_ref.shape[1]
        half = LANES // 2
        theirs = lambda r: ext_ref[r]
        ec = jnp.zeros((dates, LANES), F32)
        for p in range(edge_slots):
            mask = edge_ref[bands, p]
            xt = jnp.concatenate([edge_ref[b, p] for b in range(bands)] + [mask] * 3, axis=0).T
            for r in range(4):
                ext_ref[r, p * ROWS : (p + 1) * ROWS, :] = xt[r * ROWS : (r + 1) * ROWS]
            ec = ec + mask.astype(F32)
        ec_ref[...] = ec.astype(BF16)
        first_layer(theirs, h_ref, w1_ref, edge_slots)
        es_ref[:, 3 * half :, :] = jnp.zeros((es_ref.shape[0], half, es_ref.shape[2]), BF16)

        def settle(g, zs):
            for c in range(2):
                lanes = slice(256 * c, 256 * (c + 1))
                stats = [add_slots(zs[r], edge_slots, lanes) for r in range(4)]
                for k in range(2):
                    for r in range(2):
                        v = stats[r][k] + stats[r + 2][k]
                        for part, cut in enumerate(three_parts(v)):
                            here = slice(part * half + r * ROWS, part * half + (r + 1) * ROWS)
                            es_ref[2 * g + c, here, 256 * k : 256 * (k + 1)] = cut

        before = None
        for g in range(groups):
            zs = [second_layer(theirs, h_ref, w2_ref, g, r, edge_slots) for r in range(4)]
            if before is not None:
                settle(g - 1, before)
            before = zs
        settle(groups - 1, before)

    lane = lax.broadcasted_iota(jnp.int32, lot.shape, 1)
    four = jnp.concatenate([lot, jnp.where(lane < LANES // 2, lot, -1)], axis=1)
    row = lax.broadcasted_iota(jnp.int32, (LANES, 256), 0)
    chosen_ref[...] = ones_where(block * lots + (row // 8) * 16 + 8 * chunk + row % 8 == four)
    lot_rows = lax.broadcasted_iota(jnp.int32, (lots, LANES), 0) + block * lots
    extra = lax.dot_general(ec_ref[...], ones_where(lot_rows == lot), NT, preferred_element_type=F32)
    inverse = 1.0 / (cnt_ref[...].astype(F32) + extra)
    inv_t = jnp.concatenate([halves(inverse[:, s * LANES : (s + 1) * LANES].T)[chunk] for s in range(2)], axis=0)
    for d in range(dates):
        inv_ref[d] = jnp.broadcast_to(inv_t[:, d : d + 1], (LANES, LANES))
    first_layer(mine, h_ref, w1_ref, slots)

    def finish(g, r, z):
        here = slice(r * ROWS, (r + 1) * ROWS)
        for c in range(2):
            total, square = add_slots(z, slots, slice(256 * c, 256 * (c + 1)))
            total = total + init_ref[c, here, :256]
            square = square + init_ref[c, here, 256:]
            for k in range(2):
                d = 4 * g + 2 * c + k
                inv = inv_ref[d, here, :]
                lanes = slice(k * LANES, (k + 1) * LANES)
                average = total[:, lanes] * inv
                spread = jnp.maximum(square[:, lanes] * inv - average * average, VAR_FLOOR)
                spread = spread * lax.rsqrt(spread)
                pool_ref[d, here, :LANES] = average.astype(BF16)
                pool_ref[d, here, LANES:] = spread.astype(BF16)

    def embed(g):
        four = pool_ref[4 * g : 4 * g + 4].reshape(4 * LANES, 256)
        e = jnp.dot(four, wp_ref[...], preferred_element_type=F32)
        for k in range(4):
            d = 4 * g + k
            e_ref[d] = (e[k * LANES : (k + 1) * LANES] + code_ref[d : d + 1, :]).astype(BF16)

    before = None
    for g in range(groups):
        for r in range(4):
            z = second_layer(mine, h_ref, w2_ref, g, r, slots)
            if before is not None:
                finish(*before)
            if r == 0:
                for c in range(2):
                    init_ref[c] = jnp.dot(chosen_ref[...], es_ref[2 * g + c], preferred_element_type=F32)
            if r == 1 and g > 0:
                embed(g - 1)
            before = (g, r, z)
    finish(*before)
    embed(groups - 1)

    for k in range(0, LANES, 32):
        both = jnp.concatenate(
            [e_ref[:, k + s : k + s + 16, :].reshape(dates * 16, LANES) for s in (0, 16)], axis=1
        )
        y = jnp.dot(perm_ref[...], both, preferred_element_type=F32).astype(BF16)
        for s in range(2):
            here = slice(k // 8 + 2 * s, k // 8 + 2 * s + 2)
            out_ref[here] = y[:, s * LANES : (s + 1) * LANES].reshape(2, 8, dates, LANES)


def whole(x):
    return pl.BlockSpec(x.shape, lambda *_: (0,) * x.ndim, pipeline_mode=pl.Buffered(1))


def lay_out(pixels, counts):
    bands, slots, dates, lots = pixels.shape
    blocks = lots // 256
    laid = jax.ShapeDtypeStruct((blocks, 4, slots * ROWS, 256), BF16)
    laid_spec = pl.BlockSpec((1,) + laid.shape[1:], lambda i: (i, 0, 0, 0))
    return pl.pallas_call(
        lay_out_kernel,
        grid=(blocks,),
        in_specs=[
            pl.BlockSpec((bands, slots, dates, 256), lambda i: (0, 0, 0, i)),
            pl.BlockSpec((dates, 256), lambda i: (0, i)),
        ],
        out_specs=(laid_spec, laid_spec),
        out_shape=(laid, laid),
        compiler_params=pltpu.CompilerParams(vmem_limit_bytes=58 << 20),
        name="lay_out",
    )(pixels, counts)


def pool_lots(laid, counts, edges, lots_owned, weights, w_pool, code, peers, chunk):
    blocks, _, tall, _ = laid.shape
    edge_slots = edges.shape[1]
    dates = counts.shape[0]
    groups = dates // 4
    own = 8
    feats = w_pool.shape[1]
    fixed = (edges, lots_owned, *weights, w_pool, code)
    return pl.pallas_call(
        functools.partial(pixel_kernel, chunk=chunk),
        grid=(blocks,),
        in_specs=[
            pl.BlockSpec((1,) + laid.shape[1:], lambda i: (i, 0, 0, 0)),
            pl.BlockSpec((dates, 256), lambda i: (0, i)),
        ]
        + [whole(x) for x in fixed],
        out_specs=pl.BlockSpec((LANES // own, own, dates, feats), lambda i: (i, 0, 0, 0)),
        out_shape=jax.ShapeDtypeStruct((peers, own, dates, feats), BF16),
        scratch_shapes=[
            pltpu.VMEM((256, 512), BF16),
            pltpu.VMEM((groups, 256, 512), BF16),
            pltpu.VMEM((4, edge_slots * ROWS, 256), BF16),
            pltpu.VMEM((4, 4, tall, LANES), BF16),
            pltpu.VMEM((2 * groups, 256, 512), BF16),
            pltpu.VMEM((dates, LANES), BF16),
            pltpu.VMEM((LANES, 256), BF16),
            pltpu.VMEM((2, LANES, 512), F32),
            pltpu.VMEM((dates, LANES, LANES), F32),
            pltpu.VMEM((dates, LANES, 256), BF16),
            pltpu.VMEM((dates, LANES, LANES), BF16),
            pltpu.VMEM((256, 256), BF16),
        ],
        compiler_params=pltpu.CompilerParams(vmem_limit_bytes=58 << 20),
        name=f"pixel_pool_{chunk}",
    )(laid, counts, *fixed)


def erf_gelu(x):
    return 0.5 * x * (1.0 + lax.erf(x * (1.0 / math.sqrt(2.0))))


def norm_rows(x, gain):
    average = jnp.mean(x, axis=-1, keepdims=True)
    centered = x - average
    variance = jnp.mean(centered * centered, axis=-1, keepdims=True)
    return centered * lax.rsqrt(variance + NORM_EPS) * gain


def attention_kernel(
    e_ref, ln1_ref, wq_ref, wk_ref, wv_ref, wo_ref, ln2_ref, up_ref, down_ref, *rest, last,
):
    if last:
        first_ref, out_ref, enc_ref, q_ref, v_ref, k_ref, mix_ref = rest
    else:
        enc_ref, q_ref, v_ref, k_ref, mix_ref = rest
    peers, own, dates, width = e_ref.shape
    total = peers * dates
    head = width // HEADS
    together = q_ref.shape[0]
    tall = 256
    scale = math.log2(math.e) / math.sqrt(head)

    def rows_of(lot):
        return jnp.concatenate([e_ref[:, lot + l].reshape(total, width) for l in range(together)], axis=0).astype(F32)

    def project(lot):
        normed = norm_rows(rows_of(lot), ln1_ref[...]).astype(BF16)
        weights = jnp.concatenate([wq_ref[...], wv_ref[...]], axis=1)
        both = jnp.dot(normed, weights, preferred_element_type=F32).astype(BF16)
        keys_t = lax.dot_general(wk_ref[...].T, normed, NT, preferred_element_type=F32).astype(BF16)
        for l in range(together):
            here = slice(l * total, (l + 1) * total)
            q_ref[l] = both[here, :width]
            v_ref[l] = both[here, width:]
            k_ref[l] = keys_t[:, here]

    def mix_dates(l):
        lane = lax.broadcasted_iota(jnp.int32, (total, width), 1)
        ones = jnp.ones((total, width), BF16)
        zero = jnp.zeros((total, width), BF16)
        parts = [None] * (total // tall)
        for h in range(HEADS):
            mine = lane // head == h
            queries = jnp.where(mine, q_ref[l], zero)
            values = jnp.concatenate([jnp.where(mine, v_ref[l], zero), ones], axis=1)
            for b in range(total // tall):
                here = slice(b * tall, (b + 1) * tall)
                scores = jnp.dot(queries[here], k_ref[l], preferred_element_type=F32)
                top = jnp.max(scores, axis=1, keepdims=True) * scale
                weights = jnp.exp2(scores * scale - top).astype(BF16)
                mix = jnp.dot(weights, values, preferred_element_type=F32)
                mix = mix[:, :width] * (1.0 / mix[:, width:])
                parts[b] = mix if parts[b] is None else parts[b] + mix
        mix_ref[l] = jnp.concatenate(parts, axis=0).astype(BF16)

    def feed_forward(lot):
        mixture = mix_ref[...].reshape(together * total, width)
        carried = rows_of(lot) + jnp.dot(mixture, wo_ref[...], preferred_element_type=F32)
        normed_two = norm_rows(carried, ln2_ref[...]).astype(BF16)
        hidden = erf_gelu(jnp.dot(normed_two, up_ref[...], preferred_element_type=F32)).astype(BF16)
        encoded = (carried + jnp.dot(hidden, down_ref[...], preferred_element_type=F32)).astype(BF16)
        for l in range(together):
            enc_ref[lot + l] = encoded[l * total : (l + 1) * total].reshape(peers, dates, width)

    @pl.loop(0, own, step=together)
    def _(lot):
        project(lot)

        for l in range(together):
            mix_dates(l)

        feed_forward(lot)

    if last:
        perm = swap_rows(dates)
        for p in range(0, peers, 2):
            two = jnp.concatenate(
                [
                    jnp.concatenate([first_ref[:, p + s], enc_ref[:, p + s]], axis=0).reshape(2 * own * dates, width)
                    for s in range(2)
                ],
                axis=1,
            )
            y = jnp.dot(perm, two, preferred_element_type=F32).astype(BF16)
            for s in range(2):
                here = slice((p + s) * dates, (p + s + 1) * dates)
                out_ref[here] = y[:, s * width : (s + 1) * width].reshape(dates, 2 * own, width)


def attend(embedded, params, first=None):
    peers, own, dates, width = embedded.shape
    total = peers * dates
    together = 4
    scratch = [
        pltpu.VMEM((together, total, width), BF16),
        pltpu.VMEM((together, total, width), BF16),
        pltpu.VMEM((together, width, total), BF16),
        pltpu.VMEM((together, total, width), BF16),
    ]
    last = first is not None
    mid = (own, peers, dates, width)
    return pl.pallas_call(
        functools.partial(attention_kernel, last=last),
        out_shape=jax.ShapeDtypeStruct((total, 2 * own, width) if last else mid, BF16),
        scratch_shapes=([pltpu.VMEM(mid, BF16)] if last else []) + scratch,
        compiler_params=pltpu.CompilerParams(vmem_limit_bytes=48 << 20),
        name="attend_last" if last else "attend_first",
    )(embedded, *params, *([first] if last else []))


def position_code(day_numbers, model_width):
    lane = lax.broadcasted_iota(jnp.int32, (day_numbers.shape[0], model_width), 1)
    freq_rate = jnp.exp(-(2.0 * (lane // 2).astype(F32) / model_width) * math.log(1000.0))
    phase_angle = day_numbers.astype(F32)[:, None] * freq_rate
    return jnp.where(lane % 2 == 0, jnp.sin(phase_angle), jnp.cos(phase_angle))


def edge_kernel(pix_ref, mask_ref, out_ref):
    bands, slots = pix_ref.shape[:2]
    half = slots // 2
    for p in range(half):
        masks = [jnp.where(mask_ref[p + s * half] > 0, 1.0, 0.0) for s in range(2)]
        out_ref[bands, p] = jnp.concatenate(masks, axis=-1).astype(BF16)
        for b in range(bands):
            two = [pix_ref[b, p + s * half].astype(F32) * masks[s] for s in range(2)]
            out_ref[b, p] = jnp.concatenate(two, axis=-1).astype(BF16)


def edge_rows(edge_pixels, edge_mask):
    bands, slots, dates, blocks = edge_pixels.shape
    return pl.pallas_call(
        edge_kernel,
        out_shape=jax.ShapeDtypeStruct((bands + 1, slots // 2, dates, 2 * blocks), BF16),
        name="edge_rows",
    )(edge_pixels, edge_mask)


def per_device(
    pixels, counts, edge_pixels, edge_mask, straddle_lot, date_days,
    w_first, b_first, w_second, b_second, w_pool, b_pool,
    ln_one, w_query, w_key, w_value, w_out, ln_two, w_up, w_down,
):
    groups = lax.axis_size("group")
    peers = lax.axis_size("date")
    dates = pixels.shape[2]
    width = w_pool.shape[1]
    edges = lax.ppermute(
        edge_rows(edge_pixels, edge_mask), "group", [(i, (i + 1) % groups) for i in range(groups)]
    )
    weights = (w_first.T, b_first[None], w_second.T, b_second[None])
    own_days = lax.dynamic_slice_in_dim(date_days, lax.axis_index("date") * dates, dates)
    code = position_code(own_days, width) + b_pool
    params = (ln_one[None], w_query, w_key, w_value, w_out, ln_two[None], w_up, w_down)
    series = []
    for chunk, laid in enumerate(lay_out(pixels, counts)):
        pooled = pool_lots(laid, counts, edges, straddle_lot[None], weights, w_pool, code, peers, chunk)
        series.append(lax.all_to_all(pooled, "date", split_axis=0, concat_axis=0, tiled=True))
    return attend(series[1], params, attend(series[0], params))


def solution(mesh):
    return jax.shard_map(
        per_device,
        mesh=mesh,
        in_specs=(
            P(None, None, "date", "group"),
            P("date", "group"),
            P(None, None, "date", "group"),
            P(None, "date", "group"),
            P("group"),
        )
        + (P(),) * 15,
        out_specs=P(None, ("group", "date"), None),
        check_vma=False,
    )
```

```python
import functools
import math

import jax
import jax.numpy as jnp
from jax import lax
from jax.experimental import pallas as pl
from jax.experimental.pallas import tpu as pltpu
from jax.sharding import PartitionSpec as P

HEADS = 4
VAR_FLOOR = 0.05
NORM_EPS = 1e-05
F32 = jnp.float32
BF16 = jnp.bfloat16
LANES = 128


def relu_bf16(values):
    return jnp.maximum(values, 0.0).astype(BF16)


NT = (((1,), (1,)), ((), ()))


def ones_where(condition):
    return jnp.where(condition, 1.0, 0.0).astype(BF16)


def grid_of(shape):
    return lax.broadcasted_iota(jnp.int32, shape, 0), lax.broadcasted_iota(jnp.int32, shape, 1)


def three_parts(values):
    parts = []
    for _ in range(3):
        parts.append(values.astype(BF16))
        values = values - parts[-1].astype(F32)
    return parts


def spread_weights(wf_ref, bf_ref, ws_ref, bs_ref, w1_ref, w2_ref):
    bands, h1 = wf_ref.shape
    feats = ws_ref.shape[1]
    groups = w2_ref.shape[0]
    dates = 4 * groups
    wide = dates * h1
    row, col = grid_of((h1, wide))
    repeat = ones_where(row == col % h1)
    taps = jnp.dot(wf_ref[...], repeat, preferred_element_type=F32)
    row, col = grid_of((dates, wide))
    keep = row == col // h1
    for b in range(bands):
        line = jnp.broadcast_to(taps[b : b + 1], (dates, wide))
        w1_ref[b * dates : (b + 1) * dates, :] = jnp.where(keep, line, 0.0).astype(BF16)
    for part, values in enumerate(three_parts(jnp.broadcast_to(bf_ref[...], (dates, h1)))):
        line = jnp.dot(values, repeat, preferred_element_type=F32)
        start = (bands + part) * dates
        w1_ref[start : start + dates, :] = jnp.where(keep, line, 0.0).astype(BF16)
    stacked = jnp.concatenate([ws_ref[...].astype(F32)] * 4, axis=0)
    row_two, col_two = grid_of((4 * h1, 4 * feats))
    body = jnp.where(row_two // h1 == col_two // feats, jnp.concatenate([stacked] * 4, axis=1), 0.0).astype(BF16)
    lines = [part.astype(F32) for part in three_parts(jnp.broadcast_to(bs_ref[...], (dates, feats)))]
    lines = [jnp.concatenate([line] * 4, axis=1) for line in lines]
    row, col = grid_of((dates, 4 * feats))
    gap = 256 - 3 * dates
    for g in range(groups):
        w2_ref[g, : 4 * h1, :] = body
        w2_ref[g, 4 * h1 : gap, :] = jnp.zeros((gap - 4 * h1, 4 * feats), BF16)
        for part in range(3):
            start = gap + part * dates
            w2_ref[g, start : start + dates, :] = jnp.where(row == 4 * g + col // feats, lines[part], 0.0).astype(BF16)


def swap_rows(size):
    row = lax.broadcasted_iota(jnp.int32, (size * size, size * size), 0)
    col = lax.broadcasted_iota(jnp.int32, (size * size, size * size), 1)
    return jnp.where(col == (row % size) * size + row // size, 1.0, 0.0).astype(BF16)


ROWS = 32


def first_layer(xt, h_ref, w1_ref, count):
    def finish(r, z):
        z = relu_bf16(z)
        for g in range(4):
            h_ref[g, r, : count * ROWS, :] = z[:, g * LANES : (g + 1) * LANES]

    before = None
    for r in range(4):
        z = jnp.dot(xt(r), w1_ref[...], preferred_element_type=F32)
        if before is not None:
            finish(r - 1, before)
        before = z
    finish(3, before)


def second_layer(xt, h_ref, w2_ref, g, r, count):
    a = jnp.concatenate([h_ref[g, r, : count * ROWS, :], xt(r)[:, LANES:]], axis=1)
    return jnp.dot(a, w2_ref[g], preferred_element_type=F32)


def add_slots(z, count, lanes):
    total = square = None
    for p in range(count):
        part = jnp.maximum(z[p * ROWS : (p + 1) * ROWS, lanes], 0.0)
        total = part if total is None else total + part
        square = part * part if square is None else square + part * part
    return total, square


def halves(values):
    return [
        jnp.concatenate([values[k + 8 * c : k + 8 * c + 8] for k in range(0, LANES, 16)], axis=0) for c in range(2)
    ]


def lay_out_kernel(pix_ref, cnt_ref, first_ref, second_ref):
    bands, slots = pix_ref.shape[:2]
    counts = cnt_ref[...]
    for p in range(slots):
        mask = ones_where(counts > p)
        for side in range(2):
            lanes = slice(side * LANES, (side + 1) * LANES)
            m = mask[:, lanes]
            x = jnp.concatenate([pix_ref[b, p, :, lanes] * m for b in range(bands)] + [m] * 3, axis=0)
            for ref, xt in zip((first_ref, second_ref), halves(x.astype(F32).T)):
                xt = xt.astype(BF16)
                for r in range(2):
                    ref[0, 2 * side + r, p * ROWS : (p + 1) * ROWS, :] = xt[r * ROWS : (r + 1) * ROWS]


def pixel_kernel(
    xt_ref, cnt_ref, edge_ref, lot_ref, wf_ref, bf_ref, ws_ref, bs_ref, wp_ref, code_ref, out_ref,
    w1_ref, w2_ref, ext_ref, h_ref, es_ref, ec_ref, chosen_ref, init_ref, inv_ref, pool_ref, e_ref, perm_ref, *, chunk,
):
    block = pl.program_id(0)
    dates, lots = cnt_ref.shape
    slots = xt_ref.shape[2] // ROWS
    groups = w2_ref.shape[0]
    mine = lambda r: xt_ref[0, r]
    lot = jnp.concatenate([lot_ref[...], lot_ref[...]], axis=1)

    @pl.when(block == 0)
    def _():
        spread_weights(wf_ref, bf_ref, ws_ref, bs_ref, w1_ref, w2_ref)
        perm_ref[...] = swap_rows(dates)
        bands = edge_ref.shape[0] - 1
        edge_slots = edge_ref.shape[1]
        half = LANES // 2
        theirs = lambda r: ext_ref[r]
        ec = jnp.zeros((dates, LANES), F32)
        for p in range(edge_slots):
            mask = edge_ref[bands, p]
            xt = jnp.concatenate([edge_ref[b, p] for b in range(bands)] + [mask] * 3, axis=0).T
            for r in range(4):
                ext_ref[r, p * ROWS : (p + 1) * ROWS, :] = xt[r * ROWS : (r + 1) * ROWS]
            ec = ec + mask.astype(F32)
        ec_ref[...] = ec.astype(BF16)
        first_layer(theirs, h_ref, w1_ref, edge_slots)
        es_ref[:, 3 * half :, :] = jnp.zeros((es_ref.shape[0], half, es_ref.shape[2]), BF16)

        def settle(g, zs):
            for c in range(2):
                lanes = slice(256 * c, 256 * (c + 1))
                stats = [add_slots(zs[r], edge_slots, lanes) for r in range(4)]
                for k in range(2):
                    for r in range(2):
                        v = stats[r][k] + stats[r + 2][k]
                        for part, cut in enumerate(three_parts(v)):
                            here = slice(part * half + r * ROWS, part * half + (r + 1) * ROWS)
                            es_ref[2 * g + c, here, 256 * k : 256 * (k + 1)] = cut

        before = None
        for g in range(groups):
            zs = [second_layer(theirs, h_ref, w2_ref, g, r, edge_slots) for r in range(4)]
            if before is not None:
                settle(g - 1, before)
            before = zs
        settle(groups - 1, before)

    lane = lax.broadcasted_iota(jnp.int32, lot.shape, 1)
    four = jnp.concatenate([lot, jnp.where(lane < LANES // 2, lot, -1)], axis=1)
    row = lax.broadcasted_iota(jnp.int32, (LANES, 256), 0)
    chosen_ref[...] = ones_where(block * lots + (row // 8) * 16 + 8 * chunk + row % 8 == four)
    lot_rows = lax.broadcasted_iota(jnp.int32, (lots, LANES), 0) + block * lots
    extra = lax.dot_general(ec_ref[...], ones_where(lot_rows == lot), NT, preferred_element_type=F32)
    inverse = 1.0 / (cnt_ref[...].astype(F32) + extra)
    inv_t = jnp.concatenate([halves(inverse[:, s * LANES : (s + 1) * LANES].T)[chunk] for s in range(2)], axis=0)
    for d in range(dates):
        inv_ref[d] = jnp.broadcast_to(inv_t[:, d : d + 1], (LANES, LANES))
    first_layer(mine, h_ref, w1_ref, slots)

    def finish(g, r, z):
        here = slice(r * ROWS, (r + 1) * ROWS)
        for c in range(2):
            total, square = add_slots(z, slots, slice(256 * c, 256 * (c + 1)))
            total = total + init_ref[c, here, :256]
            square = square + init_ref[c, here, 256:]
            for k in range(2):
                d = 4 * g + 2 * c + k
                inv = inv_ref[d, here, :]
                lanes = slice(k * LANES, (k + 1) * LANES)
                average = total[:, lanes] * inv
                spread = jnp.maximum(square[:, lanes] * inv - average * average, VAR_FLOOR)
                spread = spread * lax.rsqrt(spread)
                pool_ref[d, here, :LANES] = average.astype(BF16)
                pool_ref[d, here, LANES:] = spread.astype(BF16)

    def embed(g):
        four = pool_ref[4 * g : 4 * g + 4].reshape(4 * LANES, 256)
        e = jnp.dot(four, wp_ref[...], preferred_element_type=F32)
        for k in range(4):
            d = 4 * g + k
            e_ref[d] = (e[k * LANES : (k + 1) * LANES] + code_ref[d : d + 1, :]).astype(BF16)

    before = None
    for g in range(groups):
        for r in range(4):
            z = second_layer(mine, h_ref, w2_ref, g, r, slots)
            if before is not None:
                finish(*before)
            if r == 0:
                for c in range(2):
                    init_ref[c] = jnp.dot(chosen_ref[...], es_ref[2 * g + c], preferred_element_type=F32)
            if r == 1 and g > 0:
                embed(g - 1)
            before = (g, r, z)
    finish(*before)
    embed(groups - 1)

    for k in range(0, LANES, 32):
        both = jnp.concatenate(
            [e_ref[:, k + s : k + s + 16, :].reshape(dates * 16, LANES) for s in (0, 16)], axis=1
        )
        y = jnp.dot(perm_ref[...], both, preferred_element_type=F32).astype(BF16)
        for s in range(2):
            here = slice(k // 8 + 2 * s, k // 8 + 2 * s + 2)
            out_ref[here] = y[:, s * LANES : (s + 1) * LANES].reshape(2, 8, dates, LANES)


def whole(x):
    return pl.BlockSpec(x.shape, lambda *_: (0,) * x.ndim, pipeline_mode=pl.Buffered(1))


def lay_out(pixels, counts):
    bands, slots, dates, lots = pixels.shape
    blocks = lots // 256
    laid = jax.ShapeDtypeStruct((blocks, 4, slots * ROWS, 256), BF16)
    laid_spec = pl.BlockSpec((1,) + laid.shape[1:], lambda i: (i, 0, 0, 0))
    return pl.pallas_call(
        lay_out_kernel,
        grid=(blocks,),
        in_specs=[
            pl.BlockSpec((bands, slots, dates, 256), lambda i: (0, 0, 0, i)),
            pl.BlockSpec((dates, 256), lambda i: (0, i)),
        ],
        out_specs=(laid_spec, laid_spec),
        out_shape=(laid, laid),
        compiler_params=pltpu.CompilerParams(vmem_limit_bytes=58 << 20),
        name="lay_out",
    )(pixels, counts)


def pool_lots(laid, counts, edges, lots_owned, weights, w_pool, code, peers, chunk):
    blocks, _, tall, _ = laid.shape
    edge_slots = edges.shape[1]
    dates = counts.shape[0]
    groups = dates // 4
    own = 8
    feats = w_pool.shape[1]
    fixed = (edges, lots_owned, *weights, w_pool, code)
    return pl.pallas_call(
        functools.partial(pixel_kernel, chunk=chunk),
        grid=(blocks,),
        in_specs=[
            pl.BlockSpec((1,) + laid.shape[1:], lambda i: (i, 0, 0, 0)),
            pl.BlockSpec((dates, 256), lambda i: (0, i)),
        ]
        + [whole(x) for x in fixed],
        out_specs=pl.BlockSpec((LANES // own, own, dates, feats), lambda i: (i, 0, 0, 0)),
        out_shape=jax.ShapeDtypeStruct((peers, own, dates, feats), BF16),
        scratch_shapes=[
            pltpu.VMEM((256, 512), BF16),
            pltpu.VMEM((groups, 256, 512), BF16),
            pltpu.VMEM((4, edge_slots * ROWS, 256), BF16),
            pltpu.VMEM((4, 4, tall, LANES), BF16),
            pltpu.VMEM((2 * groups, 256, 512), BF16),
            pltpu.VMEM((dates, LANES), BF16),
            pltpu.VMEM((LANES, 256), BF16),
            pltpu.VMEM((2, LANES, 512), F32),
            pltpu.VMEM((dates, LANES, LANES), F32),
            pltpu.VMEM((dates, LANES, 256), BF16),
            pltpu.VMEM((dates, LANES, LANES), BF16),
            pltpu.VMEM((256, 256), BF16),
        ],
        compiler_params=pltpu.CompilerParams(vmem_limit_bytes=52 << 20),
        name=f"pixel_pool_{chunk}",
    )(laid, counts, *fixed)


def erf_gelu(x):
    return 0.5 * x * (1.0 + lax.erf(x * (1.0 / math.sqrt(2.0))))


def norm_rows(x, gain):
    average = jnp.mean(x, axis=-1, keepdims=True)
    centered = x - average
    variance = jnp.mean(centered * centered, axis=-1, keepdims=True)
    return centered * lax.rsqrt(variance + NORM_EPS) * gain


def attention_kernel(
    e_ref, ln1_ref, wq_ref, wk_ref, wv_ref, wo_ref, ln2_ref, up_ref, down_ref, *rest, last,
):
    if last:
        first_ref, out_ref, enc_ref, q_ref, v_ref, k_ref, mix_ref = rest
    else:
        enc_ref, q_ref, v_ref, k_ref, mix_ref = rest
    peers, own, dates, width = e_ref.shape
    total = peers * dates
    head = width // HEADS
    together = q_ref.shape[0]
    tall = 512
    scale = math.log2(math.e) / math.sqrt(head)

    def rows_of(lot):
        return jnp.concatenate([e_ref[:, lot + l].reshape(total, width) for l in range(together)], axis=0).astype(F32)

    def project(lot):
        normed = norm_rows(rows_of(lot), ln1_ref[...]).astype(BF16)
        weights = jnp.concatenate([wq_ref[...], wv_ref[...]], axis=1)
        both = jnp.dot(normed, weights, preferred_element_type=F32).astype(BF16)
        keys_t = lax.dot_general(wk_ref[...].T, normed, NT, preferred_element_type=F32).astype(BF16)
        for l in range(together):
            here = slice(l * total, (l + 1) * total)
            q_ref[l] = both[here, :width]
            v_ref[l] = both[here, width:]
            k_ref[l] = keys_t[:, here]

    def mix_dates(l):
        lane = lax.broadcasted_iota(jnp.int32, (total, width), 1)
        ones = jnp.ones((total, width), BF16)
        zero = jnp.zeros((total, width), BF16)
        parts = [None] * (total // tall)
        for h in range(HEADS):
            mine = lane // head == h
            queries = jnp.where(mine, q_ref[l], zero)
            values = jnp.concatenate([jnp.where(mine, v_ref[l], zero), ones], axis=1)
            for b in range(total // tall):
                here = slice(b * tall, (b + 1) * tall)
                scores = jnp.dot(queries[here], k_ref[l], preferred_element_type=F32)
                top = jnp.max(scores, axis=1, keepdims=True) * scale
                weights = jnp.exp2(scores * scale - top).astype(BF16)
                mix = jnp.dot(weights, values, preferred_element_type=F32)
                mix = mix[:, :width] * (1.0 / mix[:, width:])
                parts[b] = mix if parts[b] is None else parts[b] + mix
        mix_ref[l] = jnp.concatenate(parts, axis=0).astype(BF16)

    def feed_forward(lot):
        mixture = mix_ref[...].reshape(together * total, width)
        carried = rows_of(lot) + jnp.dot(mixture, wo_ref[...], preferred_element_type=F32)
        normed_two = norm_rows(carried, ln2_ref[...]).astype(BF16)
        hidden = erf_gelu(jnp.dot(normed_two, up_ref[...], preferred_element_type=F32)).astype(BF16)
        encoded = (carried + jnp.dot(hidden, down_ref[...], preferred_element_type=F32)).astype(BF16)
        for l in range(together):
            enc_ref[lot + l] = encoded[l * total : (l + 1) * total].reshape(peers, dates, width)

    @pl.loop(0, own, step=together)
    def _(lot):
        project(lot)

        for l in range(together):
            mix_dates(l)

        feed_forward(lot)

    if last:
        perm = swap_rows(dates)
        for p in range(0, peers, 2):
            two = jnp.concatenate(
                [
                    jnp.concatenate([first_ref[:, p + s], enc_ref[:, p + s]], axis=0).reshape(2 * own * dates, width)
                    for s in range(2)
                ],
                axis=1,
            )
            y = jnp.dot(perm, two, preferred_element_type=F32).astype(BF16)
            for s in range(2):
                here = slice((p + s) * dates, (p + s + 1) * dates)
                out_ref[here] = y[:, s * width : (s + 1) * width].reshape(dates, 2 * own, width)


def attend(embedded, params, first=None):
    peers, own, dates, width = embedded.shape
    total = peers * dates
    together = 4
    scratch = [
        pltpu.VMEM((together, total, width), BF16),
        pltpu.VMEM((together, total, width), BF16),
        pltpu.VMEM((together, width, total), BF16),
        pltpu.VMEM((together, total, width), BF16),
    ]
    last = first is not None
    mid = (own, peers, dates, width)
    return pl.pallas_call(
        functools.partial(attention_kernel, last=last),
        out_shape=jax.ShapeDtypeStruct((total, 2 * own, width) if last else mid, BF16),
        scratch_shapes=([pltpu.VMEM(mid, BF16)] if last else []) + scratch,
        compiler_params=pltpu.CompilerParams(vmem_limit_bytes=48 << 20),
        name="attend_last" if last else "attend_first",
    )(embedded, *params, *([first] if last else []))


def position_code(day_numbers, model_width):
    lane = lax.broadcasted_iota(jnp.int32, (day_numbers.shape[0], model_width), 1)
    freq_rate = jnp.exp(-(2.0 * (lane // 2).astype(F32) / model_width) * math.log(1000.0))
    phase_angle = day_numbers.astype(F32)[:, None] * freq_rate
    return jnp.where(lane % 2 == 0, jnp.sin(phase_angle), jnp.cos(phase_angle))


def edge_kernel(pix_ref, mask_ref, out_ref):
    bands, slots = pix_ref.shape[:2]
    half = slots // 2
    for p in range(half):
        masks = [jnp.where(mask_ref[p + s * half] > 0, 1.0, 0.0) for s in range(2)]
        out_ref[bands, p] = jnp.concatenate(masks, axis=-1).astype(BF16)
        for b in range(bands):
            two = [pix_ref[b, p + s * half].astype(F32) * masks[s] for s in range(2)]
            out_ref[b, p] = jnp.concatenate(two, axis=-1).astype(BF16)


def edge_rows(edge_pixels, edge_mask):
    bands, slots, dates, blocks = edge_pixels.shape
    return pl.pallas_call(
        edge_kernel,
        out_shape=jax.ShapeDtypeStruct((bands + 1, slots // 2, dates, 2 * blocks), BF16),
        name="edge_rows",
    )(edge_pixels, edge_mask)


def per_device(
    pixels, counts, edge_pixels, edge_mask, straddle_lot, date_days,
    w_first, b_first, w_second, b_second, w_pool, b_pool,
    ln_one, w_query, w_key, w_value, w_out, ln_two, w_up, w_down,
):
    groups = lax.axis_size("group")
    peers = lax.axis_size("date")
    dates = pixels.shape[2]
    width = w_pool.shape[1]
    edges = lax.ppermute(
        edge_rows(edge_pixels, edge_mask), "group", [(i, (i + 1) % groups) for i in range(groups)]
    )
    weights = (w_first.T, b_first[None], w_second.T, b_second[None])
    own_days = lax.dynamic_slice_in_dim(date_days, lax.axis_index("date") * dates, dates)
    code = position_code(own_days, width) + b_pool
    params = (ln_one[None], w_query, w_key, w_value, w_out, ln_two[None], w_up, w_down)
    series = []
    for chunk, laid in enumerate(lay_out(pixels, counts)):
        pooled = pool_lots(laid, counts, edges, straddle_lot[None], weights, w_pool, code, peers, chunk)
        series.append(lax.all_to_all(pooled, "date", split_axis=0, concat_axis=0, tiled=True))
    return attend(series[1], params, attend(series[0], params))


def solution(mesh):
    return jax.shard_map(
        per_device,
        mesh=mesh,
        in_specs=(
            P(None, None, "date", "group"),
            P("date", "group"),
            P(None, None, "date", "group"),
            P(None, "date", "group"),
            P("group"),
        )
        + (P(),) * 15,
        out_specs=P(None, ("group", "date"), None),
        check_vma=False,
    )
```
